512 devices in a mesh: user: 16 (over z_hi, y), item: 32 (over z_lo, x, core).
Axes of the slice: x: 4, y: 8, z: 8 (z_hi: 2, z_lo: 4; z = z_hi * 4 + z_lo), core: 2. Of those that a mesh axis runs over, the one named last changes fastest.
Arguments:
- item_features: bfloat16 [4096, 256], P('item'), may hold values from -6 to 6
- level_weights: bfloat16 [3, 256, 512], replicated, may hold values from -0.21875 to 0.21875
- tile_values: bfloat16 [16, 32, 24, 128, 128], P('user', 'item'), may hold values from -0.09375 to 0.09375
- tile_order: int32 [16, 384], P('user'), may hold values from 0 to 383, each once within a row
- tile_counts: int32 [16, 32], P('user'), may hold values from 1 to 24, 384 in all within a row
- cotangent: bfloat16 [8192, 512], P(('user', 'item')), may hold values from -6 to 6
Outputs:
- hidden: bfloat16 [8192, 512], P(('user', 'item'))
- item_grad: float32 [4096, 256], P('item')
- weight_grad: float32 [3, 256, 512], replicated
The draws below stay inside these ranges and needn't reach their ends.
Inputs may be any that keep to these rules, and one draw needn't show every extreme that they name: `tile_order`: each row is a permutation of all 384 slots of the group. `tile_counts`: each row sums to 384; in every row some cell holds exactly 24 tiles.
All inputs are finite; a program needn't handle non-finite values.
Results may differ from the reference program's by a relative error of at most 0.009.
Values may be sent and summed in bfloat16 or wider, within the bound.
A program may use at most 64 MiB of HBM per device.

```python
import math
import jax
import jax.numpy as jnp
import numpy as np
from jax import lax

D = 256
H = 512
LEVELS = 3
TILE = 128
UBLK = 4
ITEM_BLK = 1
ITEMS = 4096
USERS = 8192
SLOTS = 384
CAP = 24
N_USER = 16
N_ITEM = 32


def levels(key, dims, cuts, least, high):
    def one(axis_at, parts):
        draws = jax.random.uniform(jax.random.fold_in(jax.random.fold_in(key, 6), axis_at), (parts,), jnp.float32, least / len(cuts), high / len(cuts))
        return jnp.repeat(jnp.exp(draws), dims[axis_at] // parts).reshape((-1,) + (1,) * (len(dims) - axis_at - 1))

    level = one(*cuts[0])
    for cut in cuts[1:]:
        level = level * one(*cut)
    return level


def length_profile(amount, total, reach, skew):
    weights = [(1 << 20) // math.isqrt(rank ** skew) + 1 for rank in range(2, amount + 1)]
    surplus, holding = total - reach - (amount - 1), [1] * (amount - 1)
    while surplus > 0:
        candidates = [i for i in range(amount - 1) if holding[i] < reach]
        mass, budget = sum([weights[i] for i in candidates]), surplus
        for i in candidates:
            extra = min(reach - holding[i], max(1, budget * weights[i] // mass), surplus)
            holding[i] = holding[i] + extra
            surplus = surplus - extra
    return np.array([reach] + holding)


def uneven(key, number_of, total, most, skew):
    if number_of == 2:
        one = jax.random.randint(key, (), max(1, total - most), min(most, total - 1) + 1)
        return jnp.stack([one, total - one])
    tallies = jnp.asarray(length_profile(number_of, total, most, skew), jnp.int32)
    pairs = (number_of - 1) // 2
    donor, sink = tallies[1:1 + 2 * pairs:2], tallies[2:2 + 2 * pairs:2]
    room = jnp.minimum(donor - 1, most - sink)
    passed = jax.random.randint(jax.random.fold_in(key, 1), (pairs,), 0, 1 << 20) % (room + 1)
    tallies = tallies.at[1:1 + 2 * pairs:2].set(donor - passed).at[2:2 + 2 * pairs:2].set(sink + passed)
    return tallies[jax.random.permutation(jax.random.fold_in(key, 2), number_of)]


def normal_values(key, dims, width, bound, cuts=(), dtype=jnp.bfloat16):
    factor_of = levels(key, dims, cuts, -0.22, 0.18) if cuts else 1.0
    array = jax.random.normal(key, dims, jnp.float32) * width * factor_of
    return jnp.minimum(jnp.maximum(array, -bound), bound).astype(dtype)


def setup_inputs(seed: int = 0) -> dict:
    keys = jax.random.split(jax.random.key(seed), 7)
    item_features = normal_values(keys[0], (ITEMS, D), 1.0, 6.0, ((0, 32),))
    level_weights = normal_values(keys[1], (LEVELS, D, H), (LEVELS * D) ** -0.5, 0.21875)
    tile_values = normal_values(keys[2], (N_USER, N_ITEM, CAP, TILE, TILE), ITEMS ** -0.5, 0.09375, ((0, 16), (1, 32)))
    tile_order = jax.vmap(lambda own: jax.random.permutation(own, SLOTS))(jax.random.split(keys[3], N_USER)).reshape((N_USER, SLOTS)).astype(jnp.int32)
    tile_counts = jax.vmap(lambda own: uneven(own, N_ITEM, SLOTS, CAP, 2))(jax.random.split(keys[4], N_USER)).reshape((N_USER, N_ITEM)).astype(jnp.int32)
    cotangent = normal_values(keys[5], (USERS, H), 1.0, 6.0, ((0, 512),))
    return {"item_features": item_features, "level_weights": level_weights, "tile_values": tile_values, "tile_order": tile_order, "tile_counts": tile_counts, "cotangent": cotangent}


def silu_slope(values):
    sigmoid_v = jax.nn.sigmoid(values)
    return sigmoid_v * (1.0 + values * (1.0 - sigmoid_v))

def reference(item_features, level_weights, tile_values, tile_order, tile_counts, cotangent):
    block_count = ITEM_BLK * N_ITEM
    group_rows = UBLK * TILE
    weights_wide = level_weights.astype(jnp.float32)
    cot_groups = cotangent.reshape(N_USER, group_rows, H)

    def cell_lists(order_row, count_row):
        before = (jnp.cumsum(count_row) - count_row).astype(jnp.int32)
        padded = jnp.concatenate([order_row.astype(jnp.int32), jnp.zeros((CAP,), jnp.int32)])
        slot_ids = jax.vmap(lambda offset: lax.dynamic_slice(padded, (offset,), (CAP,)))(before)
        live_slots = jnp.arange(CAP)[None, :] < count_row[:, None]
        return (slot_ids, live_slots)

    def decode(slot_id):
        level_of = slot_id // (UBLK * block_count)
        user_block = slot_id // block_count % UBLK
        item_block = slot_id % block_count
        return (level_of, user_block, item_block)

    def group_pass(inputs):
        tiles_group, order_row, count_row, cot_rows = inputs
        slot_ids, live_slots = cell_lists(order_row, count_row)

        def cell_forward(tiles_cell, slots_cell, live_cell):

            def advance(running, position):
                level_of, user_block, item_block = decode(slots_cell[position])
                features = lax.dynamic_slice_in_dim(item_features, (item_block * TILE).astype(jnp.int32), TILE, 0)
                product = jnp.dot(tiles_cell[position], features, preferred_element_type=jnp.float32)
                product = product * live_cell[position].astype(jnp.float32)
                first_row = ((level_of * UBLK + user_block) * TILE).astype(jnp.int32)
                current = lax.dynamic_slice_in_dim(running, first_row, TILE, 0)
                return (lax.dynamic_update_slice_in_dim(running, current + product, first_row, 0), None)
            start_value = jnp.zeros((LEVELS * group_rows, D), jnp.float32)
            running, unused = lax.scan(advance, start_value, jnp.arange(CAP))
            return running.astype(jnp.bfloat16)
        aggregates = jax.vmap(cell_forward)(tiles_group, slot_ids, live_slots)
        summed = lax.optimization_barrier(jnp.sum(aggregates.astype(jnp.float32), axis=0)).reshape(LEVELS, group_rows, D)
        pre_act = jnp.einsum('rud,rdh->uh', summed, weights_wide, precision=lax.Precision.HIGHEST)
        hidden = jax.nn.silu(pre_act).astype(jnp.bfloat16)
        slope_rows = (cot_rows.astype(jnp.float32) * silu_slope(pre_act)).astype(jnp.bfloat16)
        slope_wide = slope_rows.astype(jnp.float32)
        grad_terms = jnp.einsum('rud,uh->rdh', summed, slope_wide, precision=lax.Precision.HIGHEST)
        back_rows = jnp.einsum('uh,rdh->rud', slope_wide, weights_wide, precision=lax.Precision.HIGHEST)
        back_rows = back_rows.astype(jnp.bfloat16).reshape(LEVELS * group_rows, D)

        def cell_backward(tiles_cell, slots_cell, live_cell):

            def advance(running, position):
                level_of, user_block, item_block = decode(slots_cell[position])
                first_row = ((level_of * UBLK + user_block) * TILE).astype(jnp.int32)
                rows_back = lax.dynamic_slice_in_dim(back_rows, first_row, TILE, 0)
                product = jnp.dot(tiles_cell[position].T, rows_back, preferred_element_type=jnp.float32)
                product = product * live_cell[position].astype(jnp.float32)
                item_row = (item_block * TILE).astype(jnp.int32)
                current = lax.dynamic_slice_in_dim(running, item_row, TILE, 0)
                return (lax.dynamic_update_slice_in_dim(running, current + product, item_row, 0), None)
            start_value = jnp.zeros((block_count * TILE, D), jnp.float32)
            running, unused = lax.scan(advance, start_value, jnp.arange(CAP))
            return running
        item_parts = jax.vmap(cell_backward)(tiles_group, slot_ids, live_slots)
        item_total = lax.optimization_barrier(jnp.sum(item_parts, axis=0))
        return (hidden, grad_terms, item_total)
    outputs = lax.map(group_pass, (tile_values, tile_order, tile_counts, cot_groups))
    hidden_all = outputs[0].reshape(USERS, H)
    weight_grad = lax.optimization_barrier(jnp.sum(outputs[1], axis=0)) / jnp.sqrt(jnp.float32(USERS))
    item_grad = lax.optimization_barrier(jnp.sum(outputs[2], axis=0))
    return (hidden_all, item_grad, weight_grad)
```

```python
import functools

import jax
import jax.numpy as jnp
from jax import lax
from jax.experimental import pallas as pl
from jax.experimental.pallas import tpu as pltpu
from jax.sharding import PartitionSpec as P

MESH = pl.DeviceIdType.MESH
BF = jnp.bfloat16
F32 = jnp.float32
NX, NZ, NC, NY, NH = 4, 4, 2, 8, 2
TILE, D, H, LEVELS, UBLK, CAP = 128, 256, 512, 3, 4, 24
BLOCKS = NX * NZ * NC
SHARE = UBLK * TILE // BLOCKS
WROWS = LEVELS * D // (NX * NC)


class Place:
    def __init__(self):
        item = lax.axis_index("item")
        user = lax.axis_index("user")
        self.c = lax.rem(item, NC)
        self.x = lax.rem(lax.div(item, NC), NX)
        self.zl = lax.div(item, NC * NX)
        self.y = lax.rem(user, NY)
        self.zh = lax.div(user, NY)

    def dev(self, zh=None, y=None, zl=None, x=None, c=None):
        pick = lambda value, own: own if value is None else value
        user = pick(zh, self.zh) * NY + pick(y, self.y)
        item = (pick(zl, self.zl) * NX + pick(x, self.x)) * NC + pick(c, self.c)
        return (user, item)

    def xo(self, k):
        return lax.rem(self.x + (k + NX), NX)

    def zo(self, k):
        return lax.rem(self.zl + (k + NZ), NZ)

    def yo(self, k):
        return lax.rem(self.y + (k + NY), NY)

    def to_x(self, k):
        return self.dev(x=self.xo(k))

    def to_z(self, k):
        return self.dev(zl=self.zo(k))

    def to_z8(self, k):
        z = lax.rem(self.zh * NZ + self.zl + (k + NZ * NH), NZ * NH)
        return self.dev(zh=lax.div(z, NZ), zl=lax.rem(z, NZ))

    def to_y(self, k):
        return self.dev(y=self.yo(k))

    def to_core(self):
        return self.dev(c=1 - self.c)

    def to_half(self):
        return self.dev(zh=1 - self.zh)


class Net:
    def __init__(self, send_sems, recv_sems):
        self.send_sems, self.recv_sems, self.copies = send_sems, recv_sems, []

    def send(self, src, dst, device):
        at = len(self.copies)
        copy = pltpu.make_async_remote_copy(
            src_ref=src,
            dst_ref=dst,
            send_sem=self.send_sems.at[at],
            recv_sem=self.recv_sems.at[at],
            device_id=device,
            device_id_type=MESH,
        )
        copy.start()
        self.copies.append(copy)
        return copy

    def drain(self):
        for copy in self.copies:
            copy.wait_send()


def greet(devices):
    barrier = pltpu.get_barrier_semaphore()
    for device in devices:
        pl.semaphore_signal(barrier, inc=1, device_id=device, device_id_type=MESH)
    pl.semaphore_wait(barrier, len(devices))


def wide(value):
    return value.astype(F32)


def gather_zxc(net, at, ref, split):
    c = at.c
    own = ref.at[at.zl, at.x, c]
    z_copies = [net.send(own, own, at.to_z(k)) for k in range(1, NZ)]
    steps = []
    for d in range(NZ):
        z = at.zo(-d)
        if d:
            z_copies[d - 1].wait_recv()
        block = ref.at[z, at.x, c]
        steps.append((z, net.send(block, block, at.to_x(1)), net.send(block, block, at.to_x(-1))))
    relays = []
    for z, up, down in steps:
        up.wait_recv()
        piece = split(ref.at[z, at.xo(-1), c], 1)
        first = net.send(piece, piece, at.to_x(1))
        down.wait_recv()
        piece = split(ref.at[z, at.xo(1), c], 0)
        relays.append((z, first, net.send(piece, piece, at.to_x(-1))))
    swaps = []
    for z, first, second in relays:
        first.wait_recv()
        second.wait_recv()
        row = ref.at[z, :, c]
        swaps.append(net.send(row, row, at.to_core()))
    for swap in swaps:
        swap.wait_recv()


def features_kernel(feat_ref, out_ref, local_sem, send_sems, recv_sems):
    at = Place()
    net = Net(send_sems, recv_sems)
    zl, x, c = at.zl, at.x, at.c
    keep = pltpu.make_async_copy(feat_ref, out_ref.at[zl, x, c], local_sem)
    keep.start()
    greet(
        [at.to_x(1), at.to_x(-1), at.to_z8(1), at.to_z8(-1), at.to_z8(2), at.to_z8(-2), at.to_core()]
    )
    half = TILE // 2
    quarter = half // 2

    def view(z, xx, first, rows):
        return out_ref.at[z, xx, c, first : first + rows]

    def source(z, xx, first, rows, own):
        return feat_ref.at[first : first + rows] if own else view(z, xx, first, rows)

    def z_sends(xx, base, own):
        return (
            net.send(source(zl, xx, base, half, own), view(zl, xx, base, half), at.to_z8(1)),
            net.send(source(zl, xx, base, half, own), view(zl, xx, base, half), at.to_z8(-1)),
            net.send(source(zl, xx, base, quarter, own), view(zl, xx, base, quarter), at.to_z8(2)),
            net.send(
                source(zl, xx, base + quarter, quarter, own),
                view(zl, xx, base + quarter, quarter),
                at.to_z8(-2),
            ),
        )

    def x_sends(z, base, own):
        return (
            net.send(source(z, x, base, half, own), view(z, x, base, half), at.to_x(1)),
            net.send(source(z, x, base, half, own), view(z, x, base, half), at.to_x(-1)),
        )

    def x_relays(z, base, up, down):
        up.wait_recv()
        piece = view(z, at.xo(-1), base + quarter, quarter)
        first = net.send(piece, piece, at.to_x(1))
        down.wait_recv()
        piece = view(z, at.xo(1), base, quarter)
        return first, net.send(piece, piece, at.to_x(-1))

    z_first = z_sends(x, 0, True)
    x_first = x_sends(zl, half, True)
    x_of = {0: x_sends(zl, 0, True)}
    z_of = {0: z_sends(x, half, True)}
    relay_first = x_relays(zl, half, *x_first)
    z_first[0].wait_recv()
    x_of[-1] = x_sends(at.zo(-1), 0, False)
    z_of[-1] = z_sends(at.xo(-1), half, False)
    z_first[1].wait_recv()
    x_of[1] = x_sends(at.zo(1), 0, False)
    z_of[1] = z_sends(at.xo(1), half, False)
    z_first[2].wait_recv()
    z_first[3].wait_recv()
    x_of[2] = x_sends(at.zo(2), 0, False)
    relay_first[0].wait_recv()
    relay_first[1].wait_recv()
    z_of[2] = z_sends(at.xo(2), half, False)
    relays = {}
    swaps = []
    for d in (0, -1, 1, 2):
        relays[d] = x_relays(at.zo(d), 0, *x_of[d])
        for copy in z_of[d]:
            copy.wait_recv()
        row = out_ref.at[:, at.xo(d), c, half:]
        if d == 0:
            keep.wait()
        swaps.append(net.send(row, row, at.to_core()))
    for d in (0, -1, 1, 2):
        relays[d][0].wait_recv()
        relays[d][1].wait_recv()
        row = out_ref.at[at.zo(d), :, c, :half]
        swaps.append(net.send(row, row, at.to_core()))
    for swap in swaps:
        swap.wait_recv()
    net.drain()


def tile_span(counts_ref):
    item = lax.axis_index("item")
    before = lax.fori_loop(0, item, lambda i, total: total + counts_ref[0, i], jnp.int32(0))
    return before, counts_ref[0, item]


def forward_kernel(order_ref, counts_ref, tiles_ref, feats_ref, out_ref, acc_ref):
    before, holding = tile_span(counts_ref)
    acc_ref[...] = jnp.zeros_like(acc_ref)

    @pl.loop(0, holding)
    def _(t):
        slot = order_ref[0, before + t]
        target = lax.div(slot, BLOCKS)
        acc_ref[target] += jnp.dot(
            tiles_ref[t], feats_ref[lax.rem(slot, BLOCKS)], preferred_element_type=F32
        )

    for level in range(LEVELS):
        for block in range(UBLK):
            out_ref[block * TILE : (block + 1) * TILE, level * D : (level + 1) * D] = acc_ref[
                level * UBLK + block
            ].astype(BF)


def backward_kernel(
    order_ref, counts_ref, tiles_ref, slopes_ref, weights_ref, rows_ref, out_ref, wpart_ref, back_ref, acc_ref
):
    item = lax.axis_index("item")
    zl = lax.div(item, NC * NX)
    across = lax.rem(item, NC * NX)
    column = pl.ds(pl.multiple_of(zl * TILE, TILE), TILE)
    mine = jnp.concatenate(
        [
            slopes_ref[pl.ds(pl.multiple_of((z * NC * NX + across) * SHARE, SHARE), SHARE), column]
            for z in range(NZ)
        ],
        axis=0,
    )
    wpart_ref[...] = lax.dot_general(
        rows_ref[...], mine, (((0,), (0,)), ((), ())), preferred_element_type=F32
    ).astype(BF)
    before, holding = tile_span(counts_ref)
    acc_ref[...] = jnp.zeros_like(acc_ref)
    for level in range(LEVELS):
        for block in range(UBLK):
            back_ref[level * UBLK + block] = lax.dot_general(
                slopes_ref[block * TILE : (block + 1) * TILE],
                weights_ref[level * D : (level + 1) * D],
                (((1,), (1,)), ((), ())),
                preferred_element_type=F32,
            ).astype(BF)

    @pl.loop(0, holding)
    def _(t):
        slot = order_ref[0, before + t]
        block = lax.rem(slot, BLOCKS)
        acc_ref[block] += lax.dot_general(
            tiles_ref[t],
            back_ref[lax.div(slot, BLOCKS)],
            (((0,), (0,)), ((), ())),
            preferred_element_type=F32,
        )

    out_ref[...] = acc_ref[...].astype(BF)


def sum_core(net, at, src, landed):
    order = (2, 1, -1, 0)
    return [
        (k, net.send(src.at[:, at.xo(k), 1 - at.c], landed.at[:, at.xo(k)], at.to_core()))
        for k in order
    ]


def hidden_kernel(
    agg_ref,
    weights_ref,
    cot_ref,
    hidden_ref,
    slopes_ref,
    rows_ref,
    core_in,
    part,
    up_half,
    down_half,
    up_in,
    down_in,
    mid,
    z_in,
    send_sems,
    recv_sems,
):
    at = Place()
    net = Net(send_sems, recv_sems)
    zl, x, c = at.zl, at.x, at.c
    greet([at.to_core(), at.to_x(1), at.to_x(-1)] + [at.to_z(k) for k in range(1, NZ)])
    low, high = slice(0, NZ // 2), slice(NZ // 2, NZ)
    for k, copy in sum_core(net, at, agg_ref, core_in):
        copy.wait_recv()
        xx = at.xo(k)
        part[:, xx] = (wide(agg_ref[:, xx, c]) + wide(core_in[:, xx])).astype(BF)
        if k == 2:
            up_first = net.send(part.at[low, xx], up_half, at.to_x(1))
            down_first = net.send(part.at[high, xx], down_half, at.to_x(-1))
        elif k == 1:
            up_high = net.send(part.at[high, xx], up_in.at[high], at.to_x(1))
        elif k == -1:
            down_low = net.send(part.at[low, xx], down_in.at[low], at.to_x(-1))
    up_first.wait_recv()
    xx = at.xo(1)
    part[low, xx] = (wide(part[low, xx]) + wide(up_half[...])).astype(BF)
    up_low = net.send(part.at[low, xx], up_in.at[low], at.to_x(1))
    down_first.wait_recv()
    xx = at.xo(-1)
    part[high, xx] = (wide(part[high, xx]) + wide(down_half[...])).astype(BF)
    down_high = net.send(part.at[high, xx], down_in.at[high], at.to_x(-1))
    for copy in (up_high, down_low, up_low, down_high):
        copy.wait_recv()
    mid[...] = (wide(part[:, x]) + wide(up_in[...]) + wide(down_in[...])).astype(BF)
    z_copies = [net.send(mid.at[at.zo(k)], z_in.at[k - 1], at.to_z(k)) for k in range(1, NZ)]
    total = wide(mid[zl])
    for copy in z_copies:
        copy.wait_recv()
    total = total + wide(z_in[0]) + wide(z_in[1]) + wide(z_in[2])
    upper = total.astype(BF)
    lower = (total - wide(upper)).astype(BF)
    both = jnp.dot(
        jnp.concatenate([upper, lower], axis=0), weights_ref[...], preferred_element_type=F32
    )
    pre = both[:SHARE] + both[SHARE:]
    sig = 1.0 / (1.0 + jnp.exp(-pre))
    hidden_ref[...] = (pre * sig).astype(BF)
    slopes_ref[zl, x, c] = (wide(cot_ref[...]) * (sig * (1.0 + pre * (1.0 - sig)))).astype(BF)
    rows_ref[zl] = upper
    gather_zxc(net, at, slopes_ref, lambda ref, half: ref.at[:, half * (H // 2) : (half + 1) * (H // 2)])
    row_copies = [net.send(rows_ref.at[zl], rows_ref.at[zl], at.to_z(k)) for k in range(1, NZ)]
    for copy in row_copies:
        copy.wait_recv()
    net.drain()


ROWS_X = 96
ROWS_Z = TILE - ROWS_X


def grads_kernel(
    item_ref,
    weight_ref,
    item_out,
    weight_out,
    core_in,
    part,
    up_half,
    down_half,
    up_in,
    down_in,
    mid,
    z_in,
    zz_in,
    zmid,
    zx_in,
    block,
    y_in,
    y_sum,
    h_in,
    wcore_in,
    wpart,
    wup_half,
    wdown_half,
    wup_in,
    wdown_in,
    wblock,
    wy_in,
    wy_sum,
    wh_in,
    wslice,
    send_sems,
    recv_sems,
):
    at = Place()
    net = Net(send_sems, recv_sems)
    zl, x, c, y = at.zl, at.x, at.c, at.y
    greet(
        [at.to_core(), at.to_x(1), at.to_x(-1), at.to_half()]
        + [at.to_z(k) for k in range(1, NZ)]
        + [at.to_y(k) for k in range(1, NY)]
    )
    low, high = slice(0, NZ // 2), slice(NZ // 2, NZ)
    xrows, zrows = slice(0, ROWS_X), slice(ROWS_X, TILE)
    wa, wb = slice(0, WROWS // 2), slice(WROWS // 2, WROWS)

    wcore = net.send(weight_ref.at[:, 1 - c], wcore_in, at.to_core())
    core = sum_core(net, at, item_ref, core_in)

    wcore.wait_recv()
    wpart[...] = (wide(weight_ref[:, c]) + wide(wcore_in[...])).astype(BF)
    wup_first = net.send(wpart.at[at.xo(2), wa], wup_half, at.to_x(1))
    wdown_first = net.send(wpart.at[at.xo(2), wb], wdown_half, at.to_x(-1))
    wup_high = net.send(wpart.at[at.xo(1), wb], wup_in.at[wb], at.to_x(1))
    wdown_low = net.send(wpart.at[at.xo(-1), wa], wdown_in.at[wa], at.to_x(-1))

    for k, copy in core:
        copy.wait_recv()
        xx = at.xo(k)
        part[:, xx] = (wide(item_ref[:, xx, c]) + wide(core_in[:, xx])).astype(BF)
        if k == 2:
            up_first = net.send(part.at[low, xx, xrows], up_half, at.to_x(1))
            down_first = net.send(part.at[high, xx, xrows], down_half, at.to_x(-1))
        elif k == 1:
            up_high = net.send(part.at[high, xx, xrows], up_in.at[high], at.to_x(1))
        elif k == -1:
            down_low = net.send(part.at[low, xx, xrows], down_in.at[low], at.to_x(-1))
    zz = [
        net.send(part.at[at.zo(k), :, zrows], zz_in.at[k - 1], at.to_z(k)) for k in range(1, NZ)
    ]

    wup_first.wait_recv()
    wpart[at.xo(1), wa] = (wide(wpart[at.xo(1), wa]) + wide(wup_half[...])).astype(BF)
    wup_low = net.send(wpart.at[at.xo(1), wa], wup_in.at[wa], at.to_x(1))
    wdown_first.wait_recv()
    wpart[at.xo(-1), wb] = (wide(wpart[at.xo(-1), wb]) + wide(wdown_half[...])).astype(BF)
    wdown_high = net.send(wpart.at[at.xo(-1), wb], wdown_in.at[wb], at.to_x(-1))

    up_first.wait_recv()
    xx = at.xo(1)
    part[low, xx, xrows] = (wide(part[low, xx, xrows]) + wide(up_half[...])).astype(BF)
    up_low = net.send(part.at[low, xx, xrows], up_in.at[low], at.to_x(1))
    down_first.wait_recv()
    xx = at.xo(-1)
    part[high, xx, xrows] = (wide(part[high, xx, xrows]) + wide(down_half[...])).astype(BF)
    down_high = net.send(part.at[high, xx, xrows], down_in.at[high], at.to_x(-1))

    for copy in (wup_high, wdown_low, wup_low, wdown_high):
        copy.wait_recv()
    wblock[:WROWS] = (wide(wpart[x]) + wide(wup_in[...]) + wide(wdown_in[...])).astype(BF)
    wblock[WROWS:] = jnp.zeros((TILE - WROWS, TILE), BF)
    chunk = TILE // NY

    def rows_of(ref, at_y):
        return ref.at[pl.ds(pl.multiple_of(at_y * chunk, chunk), chunk)]

    wy = [net.send(rows_of(wblock, at.yo(k)), wy_in.at[k - 1], at.to_y(k)) for k in range(1, NY)]

    for copy in zz:
        copy.wait_recv()
    zmid[...] = (
        wide(part[zl, :, zrows]) + wide(zz_in[0]) + wide(zz_in[1]) + wide(zz_in[2])
    ).astype(BF)
    za, zb = slice(0, ROWS_Z // 2), slice(ROWS_Z // 2, ROWS_Z)
    zup_first = net.send(zmid.at[at.xo(2), za], zx_in.at[0, za], at.to_x(1))
    zdown_first = net.send(zmid.at[at.xo(2), zb], zx_in.at[0, zb], at.to_x(-1))
    zup_high = net.send(zmid.at[at.xo(1), zb], zx_in.at[1, zb], at.to_x(1))
    zdown_low = net.send(zmid.at[at.xo(-1), za], zx_in.at[2, za], at.to_x(-1))

    for copy in wy:
        copy.wait_recv()
    wsum = wide(rows_of(wblock, y)[...])
    for k in range(NY - 1):
        wsum = wsum + wide(wy_in[k])
    wy_sum[...] = wsum.astype(BF)
    wh = net.send(wy_sum, wh_in, at.to_half())

    for copy in (up_high, down_low, up_low, down_high):
        copy.wait_recv()
    mid[...] = (wide(part[:, x, xrows]) + wide(up_in[...]) + wide(down_in[...])).astype(BF)
    zs = [net.send(mid.at[at.zo(k)], z_in.at[k - 1], at.to_z(k)) for k in range(1, NZ)]
    zup_first.wait_recv()
    zmid[at.xo(1), za] = (wide(zmid[at.xo(1), za]) + wide(zx_in[0, za])).astype(BF)
    zup_low = net.send(zmid.at[at.xo(1), za], zx_in.at[1, za], at.to_x(1))
    zdown_first.wait_recv()
    zmid[at.xo(-1), zb] = (wide(zmid[at.xo(-1), zb]) + wide(zx_in[0, zb])).astype(BF)
    zdown_high = net.send(zmid.at[at.xo(-1), zb], zx_in.at[2, zb], at.to_x(-1))

    wh.wait_recv()
    rows_of(wslice, y)[...] = (wide(wy_sum[...]) + wide(wh_in[...])).astype(BF)
    wyg = [net.send(rows_of(wslice, y), rows_of(wslice, y), at.to_y(k)) for k in range(1, NY)]

    for copy in (zup_high, zdown_low, zup_low, zdown_high):
        copy.wait_recv()
    block[zrows] = (wide(zmid[x]) + wide(zx_in[1]) + wide(zx_in[2])).astype(BF)
    for copy in zs:
        copy.wait_recv()
    block[xrows] = (wide(mid[zl]) + wide(z_in[0]) + wide(z_in[1]) + wide(z_in[2])).astype(BF)
    ys = [net.send(rows_of(block, at.yo(k)), y_in.at[k - 1], at.to_y(k)) for k in range(1, NY)]

    for copy in wyg:
        copy.wait_recv()
    weight_out[zl, x, c] = wslice[:WROWS]
    own = weight_out.at[zl, x, c]
    wz = [net.send(own, own, at.to_z(k)) for k in range(1, NZ)]
    steps = [(zl, net.send(own, own, at.to_x(1)), net.send(own, own, at.to_x(-1)))]

    for copy in ys:
        copy.wait_recv()
    isum = wide(rows_of(block, y)[...])
    for k in range(NY - 1):
        isum = isum + wide(y_in[k])
    y_sum[...] = isum.astype(BF)
    ih = net.send(y_sum, h_in, at.to_half())

    for d in range(1, NZ):
        wz[d - 1].wait_recv()
        z = at.zo(-d)
        piece = weight_out.at[z, x, c]
        steps.append((z, net.send(piece, piece, at.to_x(1)), net.send(piece, piece, at.to_x(-1))))

    ih.wait_recv()
    rows_of(item_out, y)[...] = (wide(y_sum[...]) + wide(h_in[...])).astype(BF)
    yg = [net.send(rows_of(item_out, y), rows_of(item_out, y), at.to_y(k)) for k in range(1, NY)]

    relays = []
    for z, up, down in steps:
        up.wait_recv()
        piece = weight_out.at[z, at.xo(-1), c, wb]
        first = net.send(piece, piece, at.to_x(1))
        down.wait_recv()
        piece = weight_out.at[z, at.xo(1), c, wa]
        relays.append((z, first, net.send(piece, piece, at.to_x(-1))))
    swaps = []
    for z, first, second in relays:
        first.wait_recv()
        second.wait_recv()
        row = weight_out.at[z, :, c]
        swaps.append(net.send(row, row, at.to_core()))
    for copy in swaps + yg:
        copy.wait_recv()
    net.drain()


VM = pl.BlockSpec(memory_space=pltpu.VMEM)
SM = pl.BlockSpec(memory_space=pltpu.SMEM)


def remote_call(kernel, ins, outs, scratch, copies, collective_id):
    return pl.pallas_call(
        kernel,
        out_shape=outs,
        in_specs=[VM] * ins,
        out_specs=jax.tree.map(lambda _: VM, outs),
        scratch_shapes=scratch
        + [pltpu.SemaphoreType.DMA((copies,)), pltpu.SemaphoreType.DMA((copies,))],
        compiler_params=pltpu.CompilerParams(collective_id=collective_id, has_side_effects=True),
    )


def shape(*dims, dtype=BF):
    return jax.ShapeDtypeStruct(dims, dtype)


def vmem(*dims, dtype=BF):
    return pltpu.VMEM(dims, dtype)


def per_device(item_features, level_weights, tile_values, tile_order, tile_counts, cotangent):
    tiles = tile_values[0, 0]
    weights = level_weights.reshape(LEVELS * D, H)
    feats = remote_call(
        features_kernel, 1, shape(NZ, NX, NC, TILE, D), [pltpu.SemaphoreType.DMA], 56, 0
    )(item_features)
    agg = pl.pallas_call(
        forward_kernel,
        out_shape=shape(UBLK * TILE, LEVELS * D),
        in_specs=[SM, SM, VM, VM],
        out_specs=VM,
        scratch_shapes=[vmem(LEVELS * UBLK, TILE, D, dtype=F32)],
    )(tile_order, tile_counts, tiles, feats.reshape(BLOCKS, TILE, D))
    wide_row = (SHARE, LEVELS * D)
    hidden, slopes, rows = remote_call(
        hidden_kernel,
        3,
        (shape(SHARE, H), shape(NZ, NX, NC, SHARE, H), shape(NZ, *wide_row)),
        [
            vmem(NZ, NX, *wide_row),
            vmem(NZ, NX, *wide_row),
            vmem(NZ // 2, *wide_row),
            vmem(NZ // 2, *wide_row),
            vmem(NZ, *wide_row),
            vmem(NZ, *wide_row),
            vmem(NZ, *wide_row),
            vmem(NZ - 1, *wide_row),
        ],
        48,
        1,
    )(agg.reshape(NZ, NX, NC, *wide_row), weights, cotangent)
    item_part, weight_part = pl.pallas_call(
        backward_kernel,
        out_shape=(shape(BLOCKS, TILE, D), shape(LEVELS * D, TILE)),
        in_specs=[SM, SM, VM, VM, VM, VM],
        out_specs=(VM, VM),
        scratch_shapes=[vmem(LEVELS * UBLK, TILE, D), vmem(BLOCKS, TILE, D, dtype=F32)],
    )(
        tile_order,
        tile_counts,
        tiles,
        slopes.reshape(UBLK * TILE, H),
        weights,
        rows.reshape(NZ * SHARE, LEVELS * D),
    )
    chunk = TILE // NY
    item_sum, weight_sum = remote_call(
        grads_kernel,
        2,
        (shape(TILE, D), shape(NZ, NX, NC, WROWS, TILE)),
        [
            vmem(NZ, NX, TILE, D),
            vmem(NZ, NX, TILE, D),
            vmem(NZ // 2, ROWS_X, D),
            vmem(NZ // 2, ROWS_X, D),
            vmem(NZ, ROWS_X, D),
            vmem(NZ, ROWS_X, D),
            vmem(NZ, ROWS_X, D),
            vmem(NZ - 1, ROWS_X, D),
            vmem(NZ - 1, NX, ROWS_Z, D),
            vmem(NX, ROWS_Z, D),
            vmem(3, ROWS_Z, D),
            vmem(TILE, D),
            vmem(NY - 1, chunk, D),
            vmem(chunk, D),
            vmem(chunk, D),
            vmem(NX, WROWS, TILE),
            vmem(NX, WROWS, TILE),
            vmem(WROWS // 2, TILE),
            vmem(WROWS // 2, TILE),
            vmem(WROWS, TILE),
            vmem(WROWS, TILE),
            vmem(TILE, TILE),
            vmem(NY - 1, chunk, TILE),
            vmem(chunk, TILE),
            vmem(chunk, TILE),
            vmem(TILE, TILE),
        ],
        96,
        2,
    )(
        item_part.reshape(NZ, NX, NC, TILE, D),
        weight_part.reshape(NX, NC, WROWS, TILE),
    )
    users_total = UBLK * TILE * lax.axis_size("user")
    weight_grad = (
        wide(weight_sum).reshape(NZ, LEVELS * D, TILE).transpose(1, 0, 2)
    ) / jnp.sqrt(jnp.float32(users_total))
    return (hidden, wide(item_sum), weight_grad.reshape(LEVELS, D, H))


def solution(mesh):
    in_specs = (
        P("item", None),
        P(),
        P("user", "item", None, None, None),
        P("user", None),
        P("user", None),
        P(("user", "item"), None),
    )
    out_specs = (P(("user", "item"), None), P("item", None), P())
    return jax.shard_map(
        per_device, mesh=mesh, in_specs=in_specs, out_specs=out_specs, check_vma=False
    )
```

```python
import functools

import jax
import jax.numpy as jnp
from jax import lax
from jax.experimental import pallas as pl
from jax.experimental.pallas import tpu as pltpu
from jax.sharding import PartitionSpec as P

MESH = pl.DeviceIdType.MESH
BF = jnp.bfloat16
F32 = jnp.float32
NX, NZ, NC, NY, NH = 4, 4, 2, 8, 2
TILE, D, H, LEVELS, UBLK, CAP = 128, 256, 512, 3, 4, 24
BLOCKS = NX * NZ * NC
SHARE = UBLK * TILE // BLOCKS
WROWS = LEVELS * D // (NX * NC)


class Place:
    def __init__(self):
        item = lax.axis_index("item")
        user = lax.axis_index("user")
        self.c = lax.rem(item, NC)
        self.x = lax.rem(lax.div(item, NC), NX)
        self.zl = lax.div(item, NC * NX)
        self.y = lax.rem(user, NY)
        self.zh = lax.div(user, NY)

    def dev(self, zh=None, y=None, zl=None, x=None, c=None):
        pick = lambda value, own: own if value is None else value
        user = pick(zh, self.zh) * NY + pick(y, self.y)
        item = (pick(zl, self.zl) * NX + pick(x, self.x)) * NC + pick(c, self.c)
        return (user, item)

    def xo(self, k):
        return lax.rem(self.x + (k + NX), NX)

    def zo(self, k):
        return lax.rem(self.zl + (k + NZ), NZ)

    def yo(self, k):
        return lax.rem(self.y + (k + NY), NY)

    def to_x(self, k):
        return self.dev(x=self.xo(k))

    def to_z(self, k):
        return self.dev(zl=self.zo(k))

    def to_z8(self, k):
        z = lax.rem(self.zh * NZ + self.zl + (k + NZ * NH), NZ * NH)
        return self.dev(zh=lax.div(z, NZ), zl=lax.rem(z, NZ))

    def to_y(self, k):
        return self.dev(y=self.yo(k))

    def to_core(self):
        return self.dev(c=1 - self.c)

    def to_half(self):
        return self.dev(zh=1 - self.zh)


class Net:
    def __init__(self, send_sems, recv_sems):
        self.send_sems, self.recv_sems, self.copies = send_sems, recv_sems, []

    def send(self, src, dst, device):
        at = len(self.copies)
        copy = pltpu.make_async_remote_copy(
            src_ref=src,
            dst_ref=dst,
            send_sem=self.send_sems.at[at],
            recv_sem=self.recv_sems.at[at],
            device_id=device,
            device_id_type=MESH,
        )
        copy.start()
        self.copies.append(copy)
        return copy

    def drain(self):
        for copy in self.copies:
            copy.wait_send()


def greet(devices):
    barrier = pltpu.get_barrier_semaphore()
    for device in devices:
        pl.semaphore_signal(barrier, inc=1, device_id=device, device_id_type=MESH)
    pl.semaphore_wait(barrier, len(devices))


def wide(value):
    return value.astype(F32)


def features_kernel(feat_ref, out_ref, local_sem, send_sems, recv_sems):
    at = Place()
    net = Net(send_sems, recv_sems)
    zl, x, c = at.zl, at.x, at.c
    keep = pltpu.make_async_copy(feat_ref, out_ref.at[zl, x, c], local_sem)
    keep.start()
    greet(
        [at.to_x(1), at.to_x(-1), at.to_z8(1), at.to_z8(-1), at.to_z8(2), at.to_z8(-2), at.to_core()]
    )
    half = TILE // 2
    quarter = half // 2

    def view(z, xx, first, rows):
        return out_ref.at[z, xx, c, first : first + rows]

    def source(z, xx, first, rows, own):
        return feat_ref.at[first : first + rows] if own else view(z, xx, first, rows)

    def z_sends(xx, base, own):
        return (
            net.send(source(zl, xx, base, half, own), view(zl, xx, base, half), at.to_z8(1)),
            net.send(source(zl, xx, base, half, own), view(zl, xx, base, half), at.to_z8(-1)),
            net.send(source(zl, xx, base, quarter, own), view(zl, xx, base, quarter), at.to_z8(2)),
            net.send(
                source(zl, xx, base + quarter, quarter, own),
                view(zl, xx, base + quarter, quarter),
                at.to_z8(-2),
            ),
        )

    def x_sends(z, base, own):
        return (
            net.send(source(z, x, base, half, own), view(z, x, base, half), at.to_x(1)),
            net.send(source(z, x, base, half, own), view(z, x, base, half), at.to_x(-1)),
        )

    def x_relays(z, base, up, down):
        up.wait_recv()
        piece = view(z, at.xo(-1), base + quarter, quarter)
        first = net.send(piece, piece, at.to_x(1))
        down.wait_recv()
        piece = view(z, at.xo(1), base, quarter)
        return first, net.send(piece, piece, at.to_x(-1))

    z_first = z_sends(x, 0, True)
    x_first = x_sends(zl, half, True)
    x_of = {0: x_sends(zl, 0, True)}
    z_of = {0: z_sends(x, half, True)}
    relay_first = x_relays(zl, half, *x_first)
    z_first[0].wait_recv()
    x_of[-1] = x_sends(at.zo(-1), 0, False)
    z_of[-1] = z_sends(at.xo(-1), half, False)
    z_first[1].wait_recv()
    x_of[1] = x_sends(at.zo(1), 0, False)
    z_of[1] = z_sends(at.xo(1), half, False)
    z_first[2].wait_recv()
    z_first[3].wait_recv()
    x_of[2] = x_sends(at.zo(2), 0, False)
    relay_first[0].wait_recv()
    relay_first[1].wait_recv()
    z_of[2] = z_sends(at.xo(2), half, False)
    relays = {}
    swaps = []
    for d in (0, -1, 1, 2):
        relays[d] = x_relays(at.zo(d), 0, *x_of[d])
        for copy in z_of[d]:
            copy.wait_recv()
        row = out_ref.at[:, at.xo(d), c, half:]
        if d == 0:
            keep.wait()
        swaps.append(net.send(row, row, at.to_core()))
    for d in (0, -1, 1, 2):
        relays[d][0].wait_recv()
        relays[d][1].wait_recv()
        row = out_ref.at[at.zo(d), :, c, :half]
        swaps.append(net.send(row, row, at.to_core()))
    for swap in swaps:
        swap.wait_recv()
    net.drain()


NONE = CAP
PREV, LAST = CAP, 2 * CAP


def forward_kernel(order_ref, counts_ref, tiles_ref, feats_ref, out_ref, meta_ref, acc_ref):
    item = lax.axis_index("item")
    before = lax.fori_loop(0, item, lambda i, total: total + counts_ref[0, i], jnp.int32(0))
    holding = counts_ref[0, item]
    acc_ref[...] = jnp.zeros_like(acc_ref)

    @pl.loop(0, BLOCKS)
    def _(b):
        meta_ref[LAST + b] = jnp.int32(NONE)

    @pl.loop(0, CAP)
    def _(t):
        live = t < holding
        slot = jnp.where(live, order_ref[0, jnp.minimum(before + t, order_ref.shape[1] - 1)], 0)
        block = lax.rem(slot, BLOCKS)
        meta_ref[t] = lax.div(slot, BLOCKS)
        meta_ref[PREV + t] = jnp.where(live, meta_ref[LAST + block], NONE)

        @pl.when(live)
        def _():
            meta_ref[LAST + block] = t

    def step(t, carry):
        live = t < holding
        slot = order_ref[0, jnp.minimum(before + t, order_ref.shape[1] - 1)]
        target = jnp.where(live, lax.div(slot, BLOCKS), LEVELS * UBLK)
        acc_ref[target] += jnp.dot(
            tiles_ref[t], feats_ref[lax.rem(slot, BLOCKS)], preferred_element_type=F32
        )
        return carry

    lax.fori_loop(0, CAP, step, 0, unroll=4)
    for level in range(LEVELS):
        for block in range(UBLK):
            out_ref[block * TILE : (block + 1) * TILE, level * D : (level + 1) * D] = acc_ref[
                level * UBLK + block
            ].astype(BF)


def finish_kernel(hidden_ref, item_ref, weight_ref, hidden_out, item_out, weight_out):
    hidden_out[...] = hidden_ref[...]
    item_out[...] = wide(item_ref[...])
    scale = 1.0 / (NH * NY * UBLK * TILE) ** 0.5
    for z in range(NZ):
        weight_out[:, z * TILE : (z + 1) * TILE] = wide(weight_ref[z]) * scale


ROWS_X = 96
ROWS_Z = TILE - ROWS_X
CHUNK = TILE // NY
X_ORDER = (2, 1, -1)
Z_ORDER = (1, 2, 3)


def exchange_kernel(
    agg_ref,
    weights_ref,
    cot_ref,
    tiles_ref,
    meta_ref,
    hidden_ref,
    item_out,
    weight_out,
    turned,
    core_in,
    part,
    x_in,
    mid,
    z_in,
    slopes,
    rows,
    back,
    accs,
    wsrc,
    wcore_in,
    wpart,
    wx_in,
    wblock,
    wy_in,
    wy_sum,
    wh_in,
    wslice,
    isrc,
    icore_in,
    ipart,
    ix_in,
    imid,
    iz_in,
    zz_in,
    zmid,
    zx_in,
    block,
    y_in,
    y_sum,
    h_in,
    send_sems,
    recv_sems,
):
    at = Place()
    net = Net(send_sems, recv_sems)
    zl, x, c, y = at.zl, at.x, at.c, at.y

    def arrived(copies):
        for copy in copies:
            copy.wait_recv()

    def rows_of(ref, at_y):
        return ref.at[pl.ds(pl.multiple_of(at_y * CHUNK, CHUNK), CHUNK)]

    greet(
        [at.to_core(), at.to_half()]
        + [at.to_x(k) for k in X_ORDER]
        + [at.to_z(k) for k in Z_ORDER]
        + [at.to_y(k) for k in range(1, NY)]
    )

    core = [
        (k, net.send(agg_ref.at[:, at.xo(k), 1 - c], core_in.at[:, at.xo(k)], at.to_core()))
        for k in X_ORDER + (0,)
    ]
    for t in range(CAP):
        turned[t] = tiles_ref[t].T
    accs[NONE] = jnp.zeros((TILE, D), F32)
    x_copies = []
    for k, copy in core:
        copy.wait_recv()
        xx = at.xo(k)
        part[:, xx] = (wide(agg_ref[:, xx, c]) + wide(core_in[:, xx])).astype(BF)
        if k:
            x_copies.append(net.send(part.at[:, xx], x_in.at[len(x_copies)], at.to_x(k)))
    arrived(x_copies)

    def x_total(index):
        total = wide(part[index, x])
        for j in range(NX - 1):
            total = total + wide(x_in[j, index])
        return total

    mid[...] = x_total(slice(None)).astype(BF)
    z_copies = [net.send(mid.at[at.zo(k)], z_in.at[k - 1], at.to_z(k)) for k in Z_ORDER]
    total = x_total(zl)
    arrived(z_copies)
    for j in range(NZ - 1):
        total = total + wide(z_in[j])

    upper = total.astype(BF)
    lower = (total - wide(upper)).astype(BF)
    both = jnp.dot(
        jnp.concatenate([upper, lower], axis=0), weights_ref[...], preferred_element_type=F32
    )
    pre = both[:SHARE] + both[SHARE:]
    sig = 1.0 / (1.0 + jnp.exp(-pre))
    hidden_ref[...] = (pre * sig).astype(BF)
    slopes[zl, x, c] = (wide(cot_ref[...]) * (sig * (1.0 + pre * (1.0 - sig)))).astype(BF)
    rows[zl] = upper

    own = slopes.at[zl, x, c]
    to_z = [net.send(own, own, at.to_z(k)) for k in Z_ORDER]
    to_x = [[net.send(own, own, at.to_x(k)) for k in X_ORDER]]
    row_copies = [net.send(rows.at[zl], rows.at[zl], at.to_z(k)) for k in Z_ORDER]
    for d in Z_ORDER:
        to_z[d - 1].wait_recv()
        piece = slopes.at[at.zo(-d), x, c]
        to_x.append([net.send(piece, piece, at.to_x(k)) for k in X_ORDER])
    arrived(row_copies)
    column = pl.ds(pl.multiple_of(zl * TILE, TILE), TILE)
    mine = jnp.concatenate([slopes[z, x, c, :, column] for z in range(NZ)], axis=0)
    wsrc[...] = (
        lax.dot_general(
            rows[...].reshape(NZ * SHARE, LEVELS * D),
            mine,
            (((0,), (0,)), ((), ())),
            preferred_element_type=F32,
        )
        .astype(BF)
        .reshape(NX, NC, WROWS, TILE)
    )
    wcore = net.send(wsrc.at[:, 1 - c], wcore_in, at.to_core())
    swaps = []
    for d in range(NZ):
        arrived(to_x[d])
        row = slopes.at[at.zo(-d), :, c]
        swaps.append(net.send(row, row, at.to_core()))

    wcore.wait_recv()
    wpart[...] = (wide(wsrc[:, c]) + wide(wcore_in[...])).astype(BF)
    wx = [net.send(wpart.at[at.xo(k)], wx_in.at[j], at.to_x(k)) for j, k in enumerate(X_ORDER)]

    for d in range(NZ):
        swaps[d].wait_recv()
        z = at.zo(-d)
        mine = slopes[z].reshape(TILE, H)
        for level in range(LEVELS):
            back[level * UBLK + z] = lax.dot_general(
                mine,
                weights_ref[level * D : (level + 1) * D],
                (((1,), (1,)), ((), ())),
                preferred_element_type=F32,
            ).astype(BF)

    def tiles_back(first, last):
        for t in range(first, last):
            accs[t] = (
                jnp.dot(turned[t], back[meta_ref[t]], preferred_element_type=F32)
                + accs[meta_ref[PREV + t]]
            )

    tiles_back(0, CAP // 2)

    arrived(wx)
    wblock[:WROWS] = (wide(wpart[x]) + wide(wx_in[0]) + wide(wx_in[1]) + wide(wx_in[2])).astype(BF)
    wblock[WROWS:] = jnp.zeros((TILE - WROWS, TILE), BF)
    wy = [net.send(rows_of(wblock, at.yo(k)), wy_in.at[k - 1], at.to_y(k)) for k in range(1, NY)]

    tiles_back(CAP // 2, CAP)

    def grads_of(z, xx, cc):
        return accs[meta_ref[LAST + (z * NX + xx) * NC + cc]]

    core = []
    for k in X_ORDER + (0,):
        xx = at.xo(k)
        for z in range(NZ):
            isrc[z, xx] = grads_of(z, xx, 1 - c).astype(BF)
        core.append((k, net.send(isrc.at[:, xx], icore_in.at[:, xx], at.to_core())))

    arrived(wy)
    wsum = wide(rows_of(wblock, y)[...])
    for k in range(NY - 1):
        wsum = wsum + wide(wy_in[k])
    wy_sum[...] = wsum
    wh = net.send(wy_sum, wh_in, at.to_half())

    xrows, zrows = slice(0, ROWS_X), slice(ROWS_X, TILE)
    x_copies = []
    for k, copy in core:
        copy.wait_recv()
        xx = at.xo(k)
        for z in range(NZ):
            ipart[z, xx] = (grads_of(z, xx, c) + wide(icore_in[z, xx])).astype(BF)
        if k:
            x_copies.append(net.send(ipart.at[:, xx, xrows], ix_in.at[len(x_copies)], at.to_x(k)))
    zz = [net.send(ipart.at[at.zo(k), :, zrows], zz_in.at[k - 1], at.to_z(k)) for k in Z_ORDER]

    wh.wait_recv()
    rows_of(wslice, y)[...] = (wy_sum[...] + wh_in[...]).astype(BF)
    wyg = [net.send(rows_of(wslice, y), rows_of(wslice, y), at.to_y(k)) for k in range(1, NY)]

    arrived(zz)
    zmid[...] = (
        wide(ipart[zl, :, zrows]) + wide(zz_in[0]) + wide(zz_in[1]) + wide(zz_in[2])
    ).astype(BF)
    zx = [net.send(zmid.at[at.xo(k)], zx_in.at[j], at.to_x(k)) for j, k in enumerate(X_ORDER)]
    arrived(x_copies)

    def ix_total(index):
        total = wide(ipart[index, x, xrows])
        for j in range(NX - 1):
            total = total + wide(ix_in[j, index])
        return total

    zs = []
    for k in Z_ORDER:
        z = at.zo(k)
        imid[z] = ix_total(z).astype(BF)
        zs.append(net.send(imid.at[z], iz_in.at[k - 1], at.to_z(k)))
    mine = ix_total(zl)

    arrived(wyg)
    weight_out[zl, x, c] = wslice[:WROWS]
    own = weight_out.at[zl, x, c]
    wz = [net.send(own, own, at.to_z(k)) for k in Z_ORDER]
    wgather = [[net.send(own, own, at.to_x(k)) for k in X_ORDER]]

    arrived(zx)
    block[zrows] = (wide(zmid[x]) + wide(zx_in[0]) + wide(zx_in[1]) + wide(zx_in[2])).astype(BF)
    arrived(zs)
    block[xrows] = (mine + wide(iz_in[0]) + wide(iz_in[1]) + wide(iz_in[2])).astype(BF)
    ys = [net.send(rows_of(block, at.yo(k)), y_in.at[k - 1], at.to_y(k)) for k in range(1, NY)]
    for d in Z_ORDER:
        wz[d - 1].wait_recv()
        piece = weight_out.at[at.zo(-d), x, c]
        wgather.append([net.send(piece, piece, at.to_x(k)) for k in X_ORDER])
    arrived(ys)
    isum = wide(rows_of(block, y)[...])
    for k in range(NY - 1):
        isum = isum + wide(y_in[k])
    y_sum[...] = isum
    ih = net.send(y_sum, h_in, at.to_half())

    swaps = []
    for d in range(NZ):
        arrived(wgather[d])
        row = weight_out.at[at.zo(-d), :, c]
        swaps.append(net.send(row, row, at.to_core()))
    ih.wait_recv()
    rows_of(item_out, y)[...] = (y_sum[...] + h_in[...]).astype(BF)
    yg = [net.send(rows_of(item_out, y), rows_of(item_out, y), at.to_y(k)) for k in range(1, NY)]
    arrived(swaps)
    arrived(yg)
    net.drain()


VM = pl.BlockSpec(memory_space=pltpu.VMEM)
SM = pl.BlockSpec(memory_space=pltpu.SMEM)
LIMIT = 28 * 1024 * 1024


def shape(*dims, dtype=BF):
    return jax.ShapeDtypeStruct(dims, dtype)


def vmem(*dims, dtype=BF):
    return pltpu.VMEM(dims, dtype)


def sems(copies):
    return [pltpu.SemaphoreType.DMA((copies,)), pltpu.SemaphoreType.DMA((copies,))]


def remote(collective_id):
    return pltpu.CompilerParams(
        collective_id=collective_id, has_side_effects=True, vmem_limit_bytes=LIMIT
    )


def per_device(item_features, level_weights, tile_values, tile_order, tile_counts, cotangent):
    tiles = tile_values[0, 0]
    weights = level_weights.reshape(LEVELS * D, H)
    feats = pl.pallas_call(
        features_kernel,
        out_shape=shape(NZ, NX, NC, TILE, D),
        in_specs=[VM],
        out_specs=VM,
        scratch_shapes=[pltpu.SemaphoreType.DMA] + sems(56),
        compiler_params=remote(0),
    )(item_features)
    wide_row = (SHARE, LEVELS * D)
    agg, meta = pl.pallas_call(
        forward_kernel,
        out_shape=(shape(UBLK * TILE, LEVELS * D), shape(2 * CAP + BLOCKS, dtype=jnp.int32)),
        in_specs=[SM, SM, VM, VM],
        out_specs=(VM, SM),
        scratch_shapes=[vmem(LEVELS * UBLK + 1, TILE, D, dtype=F32)],
        compiler_params=pltpu.CompilerParams(vmem_limit_bytes=LIMIT),
    )(tile_order, tile_counts, tiles, feats.reshape(BLOCKS, TILE, D))
    hidden, item_sum, weight_sum = pl.pallas_call(
        exchange_kernel,
        out_shape=(shape(SHARE, H), shape(TILE, D), shape(NZ, NX, NC, WROWS, TILE)),
        in_specs=[VM, VM, VM, VM, SM],
        out_specs=(VM, VM, VM),
        scratch_shapes=[
            vmem(CAP, TILE, TILE),
            vmem(NZ, NX, *wide_row),
            vmem(NZ, NX, *wide_row),
            vmem(NX - 1, NZ, *wide_row),
            vmem(NZ, *wide_row),
            vmem(NZ - 1, *wide_row),
            vmem(NZ, NX, NC, SHARE, H),
            vmem(NZ, *wide_row),
            vmem(LEVELS * UBLK, TILE, D),
            vmem(CAP + 1, TILE, D, dtype=F32),
            vmem(NX, NC, WROWS, TILE),
            vmem(NX, WROWS, TILE),
            vmem(NX, WROWS, TILE),
            vmem(NX - 1, WROWS, TILE),
            vmem(TILE, TILE),
            vmem(NY - 1, CHUNK, TILE),
            vmem(CHUNK, TILE, dtype=F32),
            vmem(CHUNK, TILE, dtype=F32),
            vmem(TILE, TILE),
            vmem(NZ, NX, TILE, D),
            vmem(NZ, NX, TILE, D),
            vmem(NZ, NX, TILE, D),
            vmem(NX - 1, NZ, ROWS_X, D),
            vmem(NZ, ROWS_X, D),
            vmem(NZ - 1, ROWS_X, D),
            vmem(NZ - 1, NX, ROWS_Z, D),
            vmem(NX, ROWS_Z, D),
            vmem(NX - 1, ROWS_Z, D),
            vmem(TILE, D),
            vmem(NY - 1, CHUNK, D),
            vmem(CHUNK, D, dtype=F32),
            vmem(CHUNK, D, dtype=F32),
        ]
        + sems(128),
        compiler_params=remote(1),
    )(agg.reshape(NZ, NX, NC, *wide_row), weights, cotangent, tiles, meta)
    hidden, item_grad, weight_grad = pl.pallas_call(
        finish_kernel,
        out_shape=(shape(SHARE, H), shape(TILE, D, dtype=F32), shape(LEVELS * D, H, dtype=F32)),
        in_specs=[VM] * 3,
        out_specs=(VM,) * 3,
        compiler_params=pltpu.CompilerParams(vmem_limit_bytes=LIMIT),
    )(hidden, item_sum, weight_sum.reshape(NZ, LEVELS * D, TILE))
    return (hidden, item_grad, weight_grad.reshape(LEVELS, D, H))


def solution(mesh):
    in_specs = (
        P("item", None),
        P(),
        P("user", "item", None, None, None),
        P("user", None),
        P("user", None),
        P(("user", "item"), None),
    )
    out_specs = (P(("user", "item"), None), P("item", None), P())
    return jax.shard_map(
        per_device, mesh=mesh, in_specs=in_specs, out_specs=out_specs, check_vma=False
    )
```

```python
import functools

import jax
import jax.numpy as jnp
from jax import lax
from jax.experimental import pallas as pl
from jax.experimental.pallas import tpu as pltpu
from jax.sharding import PartitionSpec as P

MESH = pl.DeviceIdType.MESH
BF = jnp.bfloat16
F32 = jnp.float32
NX, NZ, NC, NY, NH = 4, 4, 2, 8, 2
TILE, D, H, LEVELS, UBLK, CAP = 128, 256, 512, 3, 4, 24
BLOCKS = NX * NZ * NC
SHARE = UBLK * TILE // BLOCKS
WROWS = LEVELS * D // (NX * NC)


class Place:
    def __init__(self):
        item = lax.axis_index("item")
        user = lax.axis_index("user")
        self.c = lax.rem(item, NC)
        self.x = lax.rem(lax.div(item, NC), NX)
        self.zl = lax.div(item, NC * NX)
        self.y = lax.rem(user, NY)
        self.zh = lax.div(user, NY)

    def dev(self, zh=None, y=None, zl=None, x=None, c=None):
        pick = lambda value, own: own if value is None else value
        user = pick(zh, self.zh) * NY + pick(y, self.y)
        item = (pick(zl, self.zl) * NX + pick(x, self.x)) * NC + pick(c, self.c)
        return (user, item)

    def xo(self, k):
        return lax.rem(self.x + (k + NX), NX)

    def zo(self, k):
        return lax.rem(self.zl + (k + NZ), NZ)

    def yo(self, k):
        return lax.rem(self.y + (k + NY), NY)

    def to_x(self, k):
        return self.dev(x=self.xo(k))

    def to_z(self, k):
        return self.dev(zl=self.zo(k))

    def to_z8(self, k):
        z = lax.rem(self.zh * NZ + self.zl + (k + NZ * NH), NZ * NH)
        return self.dev(zh=lax.div(z, NZ), zl=lax.rem(z, NZ))

    def to_y(self, k):
        return self.dev(y=self.yo(k))

    def to_core(self):
        return self.dev(c=1 - self.c)

    def to_half(self):
        return self.dev(zh=1 - self.zh)


class Net:
    def __init__(self, send_sems, recv_sems):
        self.send_sems, self.recv_sems, self.copies = send_sems, recv_sems, []

    def send(self, src, dst, device):
        at = len(self.copies)
        copy = pltpu.make_async_remote_copy(
            src_ref=src,
            dst_ref=dst,
            send_sem=self.send_sems.at[at],
            recv_sem=self.recv_sems.at[at],
            device_id=device,
            device_id_type=MESH,
        )
        copy.start()
        self.copies.append(copy)
        return copy

    def drain(self):
        for copy in self.copies:
            copy.wait_send()


def greet(devices):
    barrier = pltpu.get_barrier_semaphore()
    for device in devices:
        pl.semaphore_signal(barrier, inc=1, device_id=device, device_id_type=MESH)
    pl.semaphore_wait(barrier, len(devices))


def wide(value):
    return value.astype(F32)


def finish_kernel(hidden_ref, item_ref, weight_ref, hidden_out, item_out, weight_out):
    hidden_out[...] = hidden_ref[...]
    item_out[...] = wide(item_ref[...])
    scale = 1.0 / (NH * NY * UBLK * TILE) ** 0.5
    for z in range(NZ):
        weight_out[:, z * TILE : (z + 1) * TILE] = wide(weight_ref[z]) * scale


NONE = CAP
BLK, TGT, PREV_BLK, PREV_TGT, LAST_BLK = (CAP * i for i in range(5))
LAST_TGT = LAST_BLK + BLOCKS
META = LAST_TGT + LEVELS * UBLK
ROWS_X = 96
ROWS_Z = TILE - ROWS_X
CHUNK = TILE // NY
X_ORDER = (2, 1, -1)
Z_ORDER = (1, 2, 3)


def tile_lists(order, counts, meta):
    item = lax.axis_index("item")
    before = jnp.int32(0)
    for i in range(BLOCKS):
        before = before + jnp.where(i < item, counts[0, i], 0)
    holding = counts[0, item]
    blocks, targets = [], []
    for t in range(CAP):
        slot = order[0, jnp.minimum(before + t, order.shape[1] - 1)]
        live = t < holding
        blocks.append(jnp.where(live, lax.rem(slot, BLOCKS), -1))
        targets.append(jnp.where(live, lax.div(slot, BLOCKS), -1))
        meta[BLK + t] = jnp.maximum(blocks[t], 0)
        meta[TGT + t] = jnp.maximum(targets[t], 0)
    chain(targets, meta, PREV_TGT, LAST_TGT, LEVELS * UBLK)
    return blocks


def chain(keys, meta, prev, last, number):
    for t in range(CAP):
        found = jnp.int32(NONE)
        for earlier in range(t):
            found = lax.select(keys[earlier] == keys[t], jnp.int32(earlier), found)
        meta[prev + t] = found

    def step(key, carry):
        found = jnp.int32(NONE)
        for t in range(CAP):
            found = lax.select(keys[t] == key, jnp.int32(t), found)
        meta[last + key] = found
        return carry

    lax.fori_loop(0, number, step, 0)


def exchange_kernel(
    feat_ref,
    weights_hbm,
    cot_hbm,
    tiles_hbm,
    order_hbm,
    counts_hbm,
    hidden_ref,
    item_out,
    weight_out,
    order,
    counts,
    meta_ref,
    weights_ref,
    cot_ref,
    tiles_ref,
    feats,
    turned,
    asrc,
    core_in,
    part,
    x_in,
    mid,
    z_in,
    slopes,
    rows,
    back,
    accs,
    wsrc,
    wcore_in,
    wpart,
    wx_in,
    wblock,
    wy_in,
    wy_sum,
    wh_in,
    wslice,
    isrc,
    icore_in,
    ipart,
    ix_in,
    imid,
    iz_in,
    zz_in,
    zmid,
    zx_in,
    block,
    y_in,
    y_sum,
    h_in,
    local_sems,
    send_sems,
    recv_sems,
):
    at = Place()
    net = Net(send_sems, recv_sems)
    zl, x, c, y = at.zl, at.x, at.c, at.y

    def arrived(copies):
        for copy in copies:
            copy.wait_recv()

    def rows_of(ref, at_y):
        return ref.at[pl.ds(pl.multiple_of(at_y * CHUNK, CHUNK), CHUNK)]

    loads = [
        pltpu.make_async_copy(src, dst, local_sems.at[i])
        for i, (src, dst) in enumerate(
            (
                (order_hbm, order),
                (counts_hbm, counts),
                (feat_ref, feats.at[zl, x, c]),
                (tiles_hbm, tiles_ref),
                (weights_hbm, weights_ref),
                (cot_hbm, cot_ref),
            )
        )
    ]
    for load in loads:
        load.start()
    greet(
        [at.to_core()]
        + [at.to_x(k) for k in X_ORDER]
        + [at.to_z8(k) for k in range(1, NZ * NH)]
        + [at.to_y(k) for k in range(1, NY)]
    )

    half = TILE // 2
    quarter = half // 2

    def view(z, xx, first, rows):
        return feats.at[z, xx, c, first : first + rows]

    def source(z, xx, first, rows, own):
        return feat_ref.at[first : first + rows] if own else view(z, xx, first, rows)

    def z_sends(xx, base, own):
        return (
            net.send(source(zl, xx, base, half, own), view(zl, xx, base, half), at.to_z8(1)),
            net.send(source(zl, xx, base, half, own), view(zl, xx, base, half), at.to_z8(-1)),
            net.send(source(zl, xx, base, quarter, own), view(zl, xx, base, quarter), at.to_z8(2)),
            net.send(
                source(zl, xx, base + quarter, quarter, own),
                view(zl, xx, base + quarter, quarter),
                at.to_z8(-2),
            ),
        )

    def x_sends(z, base, own):
        return (
            net.send(source(z, x, base, half, own), view(z, x, base, half), at.to_x(1)),
            net.send(source(z, x, base, half, own), view(z, x, base, half), at.to_x(-1)),
        )

    def x_relays(z, base, up, down):
        up.wait_recv()
        piece = view(z, at.xo(-1), base + quarter, quarter)
        first = net.send(piece, piece, at.to_x(1))
        down.wait_recv()
        piece = view(z, at.xo(1), base, quarter)
        return first, net.send(piece, piece, at.to_x(-1))

    z_first = z_sends(x, 0, True)
    x_first = x_sends(zl, half, True)
    x_of = {0: x_sends(zl, 0, True)}
    z_of = {0: z_sends(x, half, True)}
    loads[0].wait()
    loads[1].wait()
    blocks = tile_lists(order, counts, meta_ref)
    relay_first = x_relays(zl, half, *x_first)
    z_first[0].wait_recv()
    x_of[-1] = x_sends(at.zo(-1), 0, False)
    z_of[-1] = z_sends(at.xo(-1), half, False)
    z_first[1].wait_recv()
    x_of[1] = x_sends(at.zo(1), 0, False)
    z_of[1] = z_sends(at.xo(1), half, False)
    arrived(z_first[2:])
    x_of[2] = x_sends(at.zo(2), 0, False)
    arrived(relay_first)
    z_of[2] = z_sends(at.xo(2), half, False)
    relays = {}
    swaps = []
    loads[2].wait()
    for d in (0, -1, 1, 2):
        relays[d] = x_relays(at.zo(d), 0, *x_of[d])
        arrived(z_of[d])
        row = feats.at[:, at.xo(d), c, half:]
        swaps.append(net.send(row, row, at.to_core()))
    for d in (0, -1, 1, 2):
        arrived(relays[d])
        row = feats.at[at.zo(d), :, c, :half]
        swaps.append(net.send(row, row, at.to_core()))
    loads[3].wait()
    accs[NONE] = jnp.zeros((TILE, D), F32)
    arrived(swaps)

    for t in range(CAP):
        b = meta_ref[BLK + t]
        accs[t] = (
            jnp.dot(
                tiles_ref[t],
                feats[lax.div(b, NX * NC), lax.rem(lax.div(b, NC), NX), lax.rem(b, NC)],
                preferred_element_type=F32,
            )
            + accs[meta_ref[PREV_TGT + t]]
        )

    def agg_of(z, level, xx, cc):
        first = pl.multiple_of((xx * NC + cc) * SHARE, SHARE)
        return accs[meta_ref[LAST_TGT + level * UBLK + z], pl.ds(first, SHARE), :]

    core = []
    for k in X_ORDER + (0,):
        xx = at.xo(k)
        for z in range(NZ):
            for level in range(LEVELS):
                asrc[z, xx, :, level * D : (level + 1) * D] = agg_of(z, level, xx, 1 - c).astype(BF)
        core.append((k, net.send(asrc.at[:, xx], core_in.at[:, xx], at.to_core())))
    for t in range(CAP):
        turned[t] = tiles_ref[t].T
    x_copies = []
    for k, copy in core:
        copy.wait_recv()
        xx = at.xo(k)
        for z in range(NZ):
            for level in range(LEVELS):
                lanes = slice(level * D, (level + 1) * D)
                part[z, xx, :, lanes] = (
                    agg_of(z, level, xx, c) + wide(core_in[z, xx, :, lanes])
                ).astype(BF)
        if k:
            x_copies.append(net.send(part.at[:, xx], x_in.at[len(x_copies)], at.to_x(k)))
    chain(blocks, meta_ref, PREV_BLK, LAST_BLK, BLOCKS)
    loads[4].wait()
    loads[5].wait()
    arrived(x_copies)

    def x_total(index):
        total = wide(part[index, x])
        for j in range(NX - 1):
            total = total + wide(x_in[j, index])
        return total

    mid[...] = x_total(slice(None)).astype(BF)
    z_copies = [net.send(mid.at[at.zo(k)], z_in.at[k - 1], at.to_z(k)) for k in Z_ORDER]
    total = x_total(zl)
    arrived(z_copies)
    for j in range(NZ - 1):
        total = total + wide(z_in[j])

    upper = total.astype(BF)
    lower = (total - wide(upper)).astype(BF)
    both = jnp.dot(
        jnp.concatenate([upper, lower], axis=0), weights_ref[...], preferred_element_type=F32
    )
    pre = both[:SHARE] + both[SHARE:]
    sig = 1.0 / (1.0 + jnp.exp(-pre))
    hidden_ref[...] = (pre * sig).astype(BF)
    slopes[zl, x, c] = (wide(cot_ref[...]) * (sig * (1.0 + pre * (1.0 - sig)))).astype(BF)
    rows[zl] = upper

    own = slopes.at[zl, x, c]
    to_z = [net.send(own, own, at.to_z(k)) for k in Z_ORDER]
    to_x = [[net.send(own, own, at.to_x(k)) for k in X_ORDER]]
    row_copies = [net.send(rows.at[zl], rows.at[zl], at.to_z(k)) for k in Z_ORDER]
    for d in Z_ORDER:
        to_z[d - 1].wait_recv()
        piece = slopes.at[at.zo(-d), x, c]
        to_x.append([net.send(piece, piece, at.to_x(k)) for k in X_ORDER])
    arrived(row_copies)
    column = pl.ds(pl.multiple_of(zl * TILE, TILE), TILE)
    mine = jnp.concatenate([slopes[z, x, c, :, column] for z in range(NZ)], axis=0)
    wsrc[...] = (
        lax.dot_general(
            rows[...].reshape(NZ * SHARE, LEVELS * D),
            mine,
            (((0,), (0,)), ((), ())),
            preferred_element_type=F32,
        )
        .astype(BF)
        .reshape(NX, NC, WROWS, TILE)
    )
    wcore = net.send(wsrc.at[:, 1 - c], wcore_in, at.to_core())
    swaps = []
    for d in range(NZ):
        arrived(to_x[d])
        row = slopes.at[at.zo(-d), :, c]
        swaps.append(net.send(row, row, at.to_core()))

    wcore.wait_recv()
    wpart[...] = (wide(wsrc[:, c]) + wide(wcore_in[...])).astype(BF)
    wx = [net.send(wpart.at[at.xo(k)], wx_in.at[j], at.to_x(k)) for j, k in enumerate(X_ORDER)]

    for d in range(NZ):
        swaps[d].wait_recv()
        z = at.zo(-d)
        mine = slopes[z].reshape(TILE, H)
        for level in range(LEVELS):
            back[level * UBLK + z] = lax.dot_general(
                mine,
                weights_ref[level * D : (level + 1) * D],
                (((1,), (1,)), ((), ())),
                preferred_element_type=F32,
            ).astype(BF)

    for t in range(CAP):
        accs[t] = (
            jnp.dot(turned[t], back[meta_ref[TGT + t]], preferred_element_type=F32)
            + accs[meta_ref[PREV_BLK + t]]
        )

    def grads_of(z, xx, cc):
        return accs[meta_ref[LAST_BLK + (z * NX + xx) * NC + cc]]

    core = []
    for k in X_ORDER + (0,):
        xx = at.xo(k)
        for z in range(NZ):
            isrc[z, xx] = grads_of(z, xx, 1 - c).astype(BF)
        core.append((k, net.send(isrc.at[:, xx], icore_in.at[:, xx], at.to_core())))

    arrived(wx)
    wblock[:WROWS] = (wide(wpart[x]) + wide(wx_in[0]) + wide(wx_in[1]) + wide(wx_in[2])).astype(BF)
    wblock[WROWS:] = jnp.zeros((TILE - WROWS, TILE), BF)
    wy = [net.send(rows_of(wblock, at.yo(k)), wy_in.at[k - 1], at.to_y(k)) for k in range(1, NY)]

    xrows, zrows = slice(0, ROWS_X), slice(ROWS_X, TILE)
    x_copies = []
    for k, copy in core:
        copy.wait_recv()
        xx = at.xo(k)
        for z in range(NZ):
            ipart[z, xx] = (grads_of(z, xx, c) + wide(icore_in[z, xx])).astype(BF)
        if k:
            x_copies.append(net.send(ipart.at[:, xx, xrows], ix_in.at[len(x_copies)], at.to_x(k)))
    zz = [net.send(ipart.at[at.zo(k), :, zrows], zz_in.at[k - 1], at.to_z(k)) for k in Z_ORDER]

    arrived(wy)
    wsum = wide(rows_of(wblock, y)[...])
    for k in range(NY - 1):
        wsum = wsum + wide(wy_in[k])
    wy_sum[...] = wsum
    wh = net.send(wy_sum, wh_in, at.to_half())

    arrived(zz)
    zmid[...] = (
        wide(ipart[zl, :, zrows]) + wide(zz_in[0]) + wide(zz_in[1]) + wide(zz_in[2])
    ).astype(BF)
    zx = [net.send(zmid.at[at.xo(k)], zx_in.at[j], at.to_x(k)) for j, k in enumerate(X_ORDER)]

    wh.wait_recv()
    rows_of(wslice, y)[...] = (wy_sum[...] + wh_in[...]).astype(BF)
    wyg = [net.send(rows_of(wslice, y), rows_of(wslice, y), at.to_y(k)) for k in range(1, NY)]

    arrived(x_copies)

    def ix_total(index):
        total = wide(ipart[index, x, xrows])
        for j in range(NX - 1):
            total = total + wide(ix_in[j, index])
        return total

    zs = []
    for k in Z_ORDER:
        z = at.zo(k)
        imid[z] = ix_total(z).astype(BF)
        zs.append(net.send(imid.at[z], iz_in.at[k - 1], at.to_z(k)))
    mine = ix_total(zl)

    arrived(wyg)
    weight_out[zl, x, c] = wslice[:WROWS]
    own = weight_out.at[zl, x, c]
    wz = [net.send(own, own, at.to_z(k)) for k in Z_ORDER]
    wgather = [[net.send(own, own, at.to_x(k)) for k in X_ORDER]]

    arrived(zx)
    block[zrows] = (wide(zmid[x]) + wide(zx_in[0]) + wide(zx_in[1]) + wide(zx_in[2])).astype(BF)
    arrived(zs)
    block[xrows] = (mine + wide(iz_in[0]) + wide(iz_in[1]) + wide(iz_in[2])).astype(BF)
    ys = [net.send(rows_of(block, at.yo(k)), y_in.at[k - 1], at.to_y(k)) for k in range(1, NY)]
    for d in Z_ORDER:
        wz[d - 1].wait_recv()
        piece = weight_out.at[at.zo(-d), x, c]
        wgather.append([net.send(piece, piece, at.to_x(k)) for k in X_ORDER])
    arrived(ys)
    isum = wide(rows_of(block, y)[...])
    for k in range(NY - 1):
        isum = isum + wide(y_in[k])
    y_sum[...] = isum
    ih = net.send(y_sum, h_in, at.to_half())

    swaps = []
    for d in range(NZ):
        arrived(wgather[d])
        row = weight_out.at[at.zo(-d), :, c]
        swaps.append(net.send(row, row, at.to_core()))
    ih.wait_recv()
    rows_of(item_out, y)[...] = (y_sum[...] + h_in[...]).astype(BF)
    yg = [net.send(rows_of(item_out, y), rows_of(item_out, y), at.to_y(k)) for k in range(1, NY)]
    arrived(swaps)
    arrived(yg)
    net.drain()


VM = pl.BlockSpec(memory_space=pltpu.VMEM)
HB = pl.BlockSpec(memory_space=pltpu.HBM)
LIMIT = 60 * 1024 * 1024


def shape(*dims, dtype=BF):
    return jax.ShapeDtypeStruct(dims, dtype)


def vmem(*dims, dtype=BF):
    return pltpu.VMEM(dims, dtype)


def sems(copies):
    return [pltpu.SemaphoreType.DMA((copies,)), pltpu.SemaphoreType.DMA((copies,))]


def remote(collective_id):
    return pltpu.CompilerParams(
        collective_id=collective_id, has_side_effects=True, vmem_limit_bytes=LIMIT
    )


def per_device(item_features, level_weights, tile_values, tile_order, tile_counts, cotangent):
    tiles = tile_values[0, 0]
    weights = level_weights.reshape(LEVELS * D, H)
    wide_row = (SHARE, LEVELS * D)
    hidden, item_sum, weight_sum = pl.pallas_call(
        exchange_kernel,
        out_shape=(shape(SHARE, H), shape(TILE, D), shape(NZ, NX, NC, WROWS, TILE)),
        in_specs=[HB] * 6,
        out_specs=(VM, VM, VM),
        scratch_shapes=[
            pltpu.SMEM((1, tile_order.shape[1]), jnp.int32),
            pltpu.SMEM((1, tile_counts.shape[1]), jnp.int32),
            pltpu.SMEM((META,), jnp.int32),
            vmem(LEVELS * D, H),
            vmem(SHARE, H),
            vmem(CAP, TILE, TILE),
            vmem(NZ, NX, NC, TILE, D),
            vmem(CAP, TILE, TILE),
            vmem(NZ, NX, *wide_row),
            vmem(NZ, NX, *wide_row),
            vmem(NZ, NX, *wide_row),
            vmem(NX - 1, NZ, *wide_row),
            vmem(NZ, *wide_row),
            vmem(NZ - 1, *wide_row),
            vmem(NZ, NX, NC, SHARE, H),
            vmem(NZ, *wide_row),
            vmem(LEVELS * UBLK, TILE, D),
            vmem(CAP + 1, TILE, D, dtype=F32),
            vmem(NX, NC, WROWS, TILE),
            vmem(NX, WROWS, TILE),
            vmem(NX, WROWS, TILE),
            vmem(NX - 1, WROWS, TILE),
            vmem(TILE, TILE),
            vmem(NY - 1, CHUNK, TILE),
            vmem(CHUNK, TILE, dtype=F32),
            vmem(CHUNK, TILE, dtype=F32),
            vmem(TILE, TILE),
            vmem(NZ, NX, TILE, D),
            vmem(NZ, NX, TILE, D),
            vmem(NZ, NX, TILE, D),
            vmem(NX - 1, NZ, ROWS_X, D),
            vmem(NZ, ROWS_X, D),
            vmem(NZ - 1, ROWS_X, D),
            vmem(NZ - 1, NX, ROWS_Z, D),
            vmem(NX, ROWS_Z, D),
            vmem(NX - 1, ROWS_Z, D),
            vmem(TILE, D),
            vmem(NY - 1, CHUNK, D),
            vmem(CHUNK, D, dtype=F32),
            vmem(CHUNK, D, dtype=F32),
        ]
        + [pltpu.SemaphoreType.DMA((6,))]
        + sems(192),
        compiler_params=remote(0),
    )(item_features, weights, cotangent, tiles, tile_order, tile_counts)
    hidden, item_grad, weight_grad = pl.pallas_call(
        finish_kernel,
        out_shape=(shape(SHARE, H), shape(TILE, D, dtype=F32), shape(LEVELS * D, H, dtype=F32)),
        in_specs=[VM] * 3,
        out_specs=(VM,) * 3,
    )(hidden, item_sum, weight_sum.reshape(NZ, LEVELS * D, TILE))
    return (hidden, item_grad, weight_grad.reshape(LEVELS, D, H))


def solution(mesh):
    in_specs = (
        P("item", None),
        P(),
        P("user", "item", None, None, None),
        P("user", None),
        P("user", None),
        P(("user", "item"), None),
    )
    out_specs = (P(("user", "item"), None), P("item", None), P())
    return jax.shard_map(
        per_device, mesh=mesh, in_specs=in_specs, out_specs=out_specs, check_vma=False
    )
```

```python
import functools

import jax
import jax.numpy as jnp
from jax import lax
from jax.experimental import pallas as pl
from jax.experimental.pallas import tpu as pltpu
from jax.sharding import PartitionSpec as P

MESH = pl.DeviceIdType.MESH
BF = jnp.bfloat16
F32 = jnp.float32
NX, NZ, NC, NY, NH = 4, 4, 2, 8, 2
TILE, D, H, LEVELS, UBLK, CAP = 128, 256, 512, 3, 4, 24
BLOCKS = NX * NZ * NC
SHARE = UBLK * TILE // BLOCKS
WROWS = LEVELS * D // (NX * NC)


class Place:
    def __init__(self):
        item = lax.axis_index("item")
        user = lax.axis_index("user")
        self.c = lax.rem(item, NC)
        self.x = lax.rem(lax.div(item, NC), NX)
        self.zl = lax.div(item, NC * NX)
        self.y = lax.rem(user, NY)
        self.zh = lax.div(user, NY)

    def dev(self, zh=None, y=None, zl=None, x=None, c=None):
        pick = lambda value, own: own if value is None else value
        user = pick(zh, self.zh) * NY + pick(y, self.y)
        item = (pick(zl, self.zl) * NX + pick(x, self.x)) * NC + pick(c, self.c)
        return (user, item)

    def xo(self, k):
        return lax.rem(self.x + (k + NX), NX)

    def zo(self, k):
        return lax.rem(self.zl + (k + NZ), NZ)

    def yo(self, k):
        return lax.rem(self.y + (k + NY), NY)

    def to_x(self, k):
        return self.dev(x=self.xo(k))

    def to_z(self, k):
        return self.dev(zl=self.zo(k))

    def to_z8(self, k):
        z = lax.rem(self.zh * NZ + self.zl + (k + NZ * NH), NZ * NH)
        return self.dev(zh=lax.div(z, NZ), zl=lax.rem(z, NZ))

    def to_y(self, k):
        return self.dev(y=self.yo(k))

    def to_core(self):
        return self.dev(c=1 - self.c)

    def to_half(self):
        return self.dev(zh=1 - self.zh)


class Net:
    def __init__(self, send_sems, recv_sems):
        self.send_sems, self.recv_sems, self.copies = send_sems, recv_sems, []

    def send(self, src, dst, device):
        at = len(self.copies)
        copy = pltpu.make_async_remote_copy(
            src_ref=src,
            dst_ref=dst,
            send_sem=self.send_sems.at[at],
            recv_sem=self.recv_sems.at[at],
            device_id=device,
            device_id_type=MESH,
        )
        copy.start()
        self.copies.append(copy)
        return copy

    def drain(self):
        for copy in self.copies:
            copy.wait_send()


def greet(devices):
    barrier = pltpu.get_barrier_semaphore()
    for device in devices:
        pl.semaphore_signal(barrier, inc=1, device_id=device, device_id_type=MESH)
    pl.semaphore_wait(barrier, len(devices))


def wide(value):
    return value.astype(F32)


def finish_kernel(hidden_ref, item_ref, weight_ref, hidden_out, item_out, weight_out):
    hidden_out[...] = hidden_ref[...]
    item_out[...] = wide(item_ref[...])
    scale = 1.0 / (NH * NY * UBLK * TILE) ** 0.5
    for z in range(NZ):
        weight_out[:, z * TILE : (z + 1) * TILE] = wide(weight_ref[z]) * scale


NONE = CAP
BLK, TGT, PREV_BLK, PREV_TGT, LAST_BLK = (CAP * i for i in range(5))
LAST_TGT = LAST_BLK + BLOCKS
META = LAST_TGT + LEVELS * UBLK
ROWS_X = 80
FEAT_Z = 80
LANES_X = 512
ROWS_Z = TILE - ROWS_X
CHUNK = TILE // NY
X_ORDER = (2, 1, -1)
Z_ORDER = (1, 2, 3)


def tile_lists(order, counts, meta):
    item = lax.axis_index("item")
    before = jnp.int32(0)
    for i in range(BLOCKS):
        before = before + jnp.where(i < item, counts[0, i], 0)
    holding = counts[0, item]
    blocks, targets = [], []
    for t in range(CAP):
        slot = order[0, jnp.minimum(before + t, order.shape[1] - 1)]
        live = t < holding
        blocks.append(jnp.where(live, lax.rem(slot, BLOCKS), -1))
        targets.append(jnp.where(live, lax.div(slot, BLOCKS), -1))
        meta[BLK + t] = jnp.maximum(blocks[t], 0)
        meta[TGT + t] = jnp.maximum(targets[t], 0)
    return blocks, targets


def chain(keys, meta, prev, last, number):
    for t in range(CAP):
        found = jnp.int32(NONE)
        for earlier in range(t):
            found = lax.select(keys[earlier] == keys[t], jnp.int32(earlier), found)
        meta[prev + t] = found

    def step(key, carry):
        found = jnp.int32(NONE)
        for t in range(CAP):
            found = lax.select(keys[t] == key, jnp.int32(t), found)
        meta[last + key] = found
        return carry

    lax.fori_loop(0, number, step, 0)


def exchange_kernel(
    feat_ref,
    weights_hbm,
    cot_hbm,
    tiles_hbm,
    order_hbm,
    counts_hbm,
    hidden_ref,
    item_out,
    weight_out,
    order,
    counts,
    meta_ref,
    weights_ref,
    cot_ref,
    tiles_ref,
    feats,
    turned,
    asrc,
    core_in,
    part,
    x_in,
    mid,
    z_in,
    az_in,
    amid,
    ax_in,
    slopes,
    rows,
    back,
    accs,
    wsrc,
    wcore_in,
    wpart,
    wx_in,
    wblock,
    wy_in,
    wy_sum,
    wh_in,
    wslice,
    isrc,
    icore_in,
    ipart,
    ix_in,
    imid,
    iz_in,
    zz_in,
    zmid,
    zx_in,
    block,
    y_in,
    y_sum,
    h_in,
    local_sems,
    send_sems,
    recv_sems,
):
    at = Place()
    net = Net(send_sems, recv_sems)
    zl, x, c, y = at.zl, at.x, at.c, at.y

    def arrived(copies):
        for copy in copies:
            copy.wait_recv()

    def rows_of(ref, at_y):
        return ref.at[pl.ds(pl.multiple_of(at_y * CHUNK, CHUNK), CHUNK)]

    loads = [
        pltpu.make_async_copy(src, dst, local_sems.at[i])
        for i, (src, dst) in enumerate(
            (
                (order_hbm, order),
                (counts_hbm, counts),
                (feat_ref, feats.at[zl, x, c]),
                (tiles_hbm, tiles_ref),
                (weights_hbm, weights_ref),
                (cot_hbm, cot_ref),
            )
        )
    ]
    for load in loads:
        load.start()
    greet(
        [at.to_core()]
        + [at.to_x(k) for k in X_ORDER]
        + [at.to_z8(k) for k in range(1, NZ * NH)]
        + [at.to_y(k) for k in range(1, NY)]
    )

    first_rows, other_rows = (0, 32, FEAT_Z), (FEAT_Z, FEAT_Z + 32, TILE)

    def send_rows(z, xx, first, last, device, own):
        there = feats.at[z, xx, c, first:last]
        return net.send(feat_ref.at[first:last] if own else there, there, device)

    def z_sends(xx, cut, own, flip=False):
        low, middle, high = cut
        if flip:
            middle = low + high - middle
        return (
            send_rows(zl, xx, low, high, at.to_z8(1), own),
            send_rows(zl, xx, low, high, at.to_z8(-1), own),
            send_rows(zl, xx, low, middle, at.to_z8(2), own),
            send_rows(zl, xx, middle, high, at.to_z8(-2), own),
        )

    def x_sends(z, own):
        return (
            send_rows(z, x, 0, FEAT_Z, at.to_x(1), own),
            send_rows(z, x, 0, FEAT_Z, at.to_x(-1), own),
        )

    def x_relays(z, up, down):
        up.wait_recv()
        first = send_rows(z, at.xo(-1), 48, FEAT_Z, at.to_x(1), False)
        down.wait_recv()
        return first, send_rows(z, at.xo(1), 0, 48, at.to_x(-1), False)

    z_first = z_sends(x, first_rows, True)
    x_first = {
        -k: send_rows(zl, x, FEAT_Z, TILE, at.to_x(k), True) for k in (1, -1, 2)
    }
    x_of = {0: x_sends(zl, True)}
    z_of = {0: z_sends(x, other_rows, True)}
    loads[0].wait()
    loads[1].wait()
    blocks, targets = tile_lists(order, counts, meta_ref)
    x_first[-1].wait_recv()
    z_of[-1] = z_sends(at.xo(-1), other_rows, False)
    z_first[0].wait_recv()
    x_of[-1] = x_sends(at.zo(-1), False)
    x_first[1].wait_recv()
    z_of[1] = z_sends(at.xo(1), other_rows, False, flip=True)
    z_first[1].wait_recv()
    x_of[1] = x_sends(at.zo(1), False)
    x_first[-2].wait_recv()
    z_of[2] = z_sends(at.xo(2), other_rows, False, flip=True)
    arrived(z_first[2:])
    x_of[2] = x_sends(at.zo(2), False)
    relays = {d: x_relays(at.zo(d), *x_of[d]) for d in (0, -1)}
    loads[3].wait()
    for t in range(CAP):
        turned[t] = tiles_ref[t].T
    for d in (1, 2):
        relays[d] = x_relays(at.zo(d), *x_of[d])
    chain(targets, meta_ref, PREV_TGT, LAST_TGT, LEVELS * UBLK)
    accs[NONE] = jnp.zeros((TILE, D), F32)
    swaps = []
    loads[2].wait()
    for d in (0, -1, 1, 2):
        arrived(z_of[d])
        row = feats.at[:, at.xo(d), c, FEAT_Z:]
        swaps.append(net.send(row, row, at.to_core()))
    for d in (0, -1, 1, 2):
        arrived(relays[d])
        row = feats.at[at.zo(d), :, c, :FEAT_Z]
        swaps.append(net.send(row, row, at.to_core()))
    arrived(swaps)

    for t in range(CAP):
        b = meta_ref[BLK + t]
        accs[t] = (
            jnp.dot(
                tiles_ref[t],
                feats[lax.div(b, NX * NC), lax.rem(lax.div(b, NC), NX), lax.rem(b, NC)],
                preferred_element_type=F32,
            )
            + accs[meta_ref[PREV_TGT + t]]
        )

    def agg_of(z, level, xx, cc):
        first = pl.multiple_of((xx * NC + cc) * SHARE, SHARE)
        return accs[meta_ref[LAST_TGT + level * UBLK + z], pl.ds(first, SHARE), :]

    core = []
    for k in X_ORDER + (0,):
        xx = at.xo(k)
        for z in range(NZ):
            for level in range(LEVELS):
                asrc[z, xx, :, level * D : (level + 1) * D] = agg_of(z, level, xx, 1 - c).astype(BF)
        core.append((k, net.send(asrc.at[:, xx], core_in.at[:, xx], at.to_core())))
    xlanes, zlanes = slice(0, LANES_X), slice(LANES_X, LEVELS * D)
    x_copies = []
    for k, copy in core:
        copy.wait_recv()
        xx = at.xo(k)
        for z in range(NZ):
            for level in range(LEVELS):
                lanes = slice(level * D, (level + 1) * D)
                part[z, xx, :, lanes] = (
                    agg_of(z, level, xx, c) + wide(core_in[z, xx, :, lanes])
                ).astype(BF)
        if k:
            x_copies.append(
                net.send(part.at[:, xx, :, xlanes], x_in.at[len(x_copies)], at.to_x(k))
            )
    az = [net.send(part.at[at.zo(k), :, :, zlanes], az_in.at[k - 1], at.to_z(k)) for k in Z_ORDER]
    chain(blocks, meta_ref, PREV_BLK, LAST_BLK, BLOCKS)
    loads[4].wait()
    loads[5].wait()
    arrived(x_copies)

    def x_total(index):
        total = wide(part[index, x, :, xlanes])
        for j in range(NX - 1):
            total = total + wide(x_in[j, index])
        return total

    z_copies = []
    for k in Z_ORDER:
        mid[at.zo(k)] = x_total(at.zo(k)).astype(BF)
        z_copies.append(net.send(mid.at[at.zo(k)], z_in.at[k - 1], at.to_z(k)))
    left = x_total(zl)
    arrived(az)

    def z_total(index):
        total = wide(part[zl, index, :, zlanes])
        for j in range(NZ - 1):
            total = total + wide(az_in[j, index])
        return total

    ax = []
    for j, k in enumerate(X_ORDER):
        amid[at.xo(k)] = z_total(at.xo(k)).astype(BF)
        ax.append(net.send(amid.at[at.xo(k)], ax_in.at[j], at.to_x(k)))
    right = z_total(x)
    arrived(ax)
    for j in range(NX - 1):
        right = right + wide(ax_in[j])
    arrived(z_copies)
    for j in range(NZ - 1):
        left = left + wide(z_in[j])
    total = jnp.concatenate([left, right], axis=1)

    upper = total.astype(BF)
    lower = (total - wide(upper)).astype(BF)
    both = jnp.dot(
        jnp.concatenate([upper, lower], axis=0), weights_ref[...], preferred_element_type=F32
    )
    pre = both[:SHARE] + both[SHARE:]
    sig = 1.0 / (1.0 + jnp.exp(-pre))
    hidden_ref[...] = (pre * sig).astype(BF)
    slopes[zl, x, c] = (wide(cot_ref[...]) * (sig * (1.0 + pre * (1.0 - sig)))).astype(BF)
    rows[zl] = upper

    own = slopes.at[zl, x, c]
    to_z = [net.send(own, own, at.to_z(k)) for k in Z_ORDER]
    to_x = [[net.send(own, own, at.to_x(k)) for k in X_ORDER]]
    row_copies = [net.send(rows.at[zl], rows.at[zl], at.to_z(k)) for k in Z_ORDER]
    for d in Z_ORDER:
        to_z[d - 1].wait_recv()
        piece = slopes.at[at.zo(-d), x, c]
        to_x.append([net.send(piece, piece, at.to_x(k)) for k in X_ORDER])
    arrived(row_copies)
    column = pl.ds(pl.multiple_of(zl * TILE, TILE), TILE)
    mine = jnp.concatenate([slopes[z, x, c, :, column] for z in range(NZ)], axis=0)
    wsrc[...] = (
        lax.dot_general(
            rows[...].reshape(NZ * SHARE, LEVELS * D),
            mine,
            (((0,), (0,)), ((), ())),
            preferred_element_type=F32,
        )
        .astype(BF)
        .reshape(NX, NC, WROWS, TILE)
    )
    wcore = net.send(wsrc.at[:, 1 - c], wcore_in, at.to_core())
    swaps = []
    for d in range(NZ):
        arrived(to_x[d])
        row = slopes.at[at.zo(-d), :, c]
        swaps.append(net.send(row, row, at.to_core()))

    wcore.wait_recv()
    wpart[...] = (wide(wsrc[:, c]) + wide(wcore_in[...])).astype(BF)
    wx = [net.send(wpart.at[at.xo(k)], wx_in.at[j], at.to_x(k)) for j, k in enumerate(X_ORDER)]

    for d in range(NZ):
        swaps[d].wait_recv()
        z = at.zo(-d)
        mine = slopes[z].reshape(TILE, H)
        for level in range(LEVELS):
            back[level * UBLK + z] = lax.dot_general(
                mine,
                weights_ref[level * D : (level + 1) * D],
                (((1,), (1,)), ((), ())),
                preferred_element_type=F32,
            ).astype(BF)

    for t in range(CAP):
        accs[t] = (
            jnp.dot(turned[t], back[meta_ref[TGT + t]], preferred_element_type=F32)
            + accs[meta_ref[PREV_BLK + t]]
        )

    def grads_of(z, xx, cc):
        return accs[meta_ref[LAST_BLK + (z * NX + xx) * NC + cc]]

    core = []
    for k in X_ORDER + (0,):
        xx = at.xo(k)
        for z in range(NZ):
            isrc[z, xx] = grads_of(z, xx, 1 - c).astype(BF)
        core.append((k, net.send(isrc.at[:, xx], icore_in.at[:, xx], at.to_core())))

    arrived(wx)
    wblock[:WROWS] = (wide(wpart[x]) + wide(wx_in[0]) + wide(wx_in[1]) + wide(wx_in[2])).astype(BF)
    wblock[WROWS:] = jnp.zeros((TILE - WROWS, TILE), BF)
    wy = [net.send(rows_of(wblock, at.yo(k)), wy_in.at[k - 1], at.to_y(k)) for k in range(1, NY)]

    xrows, zrows = slice(0, ROWS_X), slice(ROWS_X, TILE)
    x_copies = []
    for k, copy in core:
        copy.wait_recv()
        xx = at.xo(k)
        for z in range(NZ):
            ipart[z, xx] = (grads_of(z, xx, c) + wide(icore_in[z, xx])).astype(BF)
        if k:
            x_copies.append(net.send(ipart.at[:, xx, xrows], ix_in.at[len(x_copies)], at.to_x(k)))
    zz = [net.send(ipart.at[at.zo(k), :, zrows], zz_in.at[k - 1], at.to_z(k)) for k in Z_ORDER]

    arrived(wy)
    wsum = wide(rows_of(wblock, y)[...])
    for k in range(NY - 1):
        wsum = wsum + wide(wy_in[k])
    wy_sum[...] = wsum
    wh = net.send(wy_sum, wh_in, at.to_half())

    arrived(zz)
    zmid[...] = (
        wide(ipart[zl, :, zrows]) + wide(zz_in[0]) + wide(zz_in[1]) + wide(zz_in[2])
    ).astype(BF)
    zx = [net.send(zmid.at[at.xo(k)], zx_in.at[j], at.to_x(k)) for j, k in enumerate(X_ORDER)]

    wh.wait_recv()
    rows_of(wslice, y)[...] = (wy_sum[...] + wh_in[...]).astype(BF)
    wyg = [net.send(rows_of(wslice, y), rows_of(wslice, y), at.to_y(k)) for k in range(1, NY)]

    arrived(x_copies)

    def ix_total(index):
        total = wide(ipart[index, x, xrows])
        for j in range(NX - 1):
            total = total + wide(ix_in[j, index])
        return total

    zs = []
    for k in Z_ORDER:
        z = at.zo(k)
        imid[z] = ix_total(z).astype(BF)
        zs.append(net.send(imid.at[z], iz_in.at[k - 1], at.to_z(k)))
    mine = ix_total(zl)

    arrived(wyg)
    weight_out[zl, x, c] = wslice[:WROWS]
    own = weight_out.at[zl, x, c]
    wz = [net.send(own, own, at.to_z(k)) for k in Z_ORDER]
    wgather = [[net.send(own, own, at.to_x(k)) for k in X_ORDER]]

    arrived(zx)
    block[zrows] = (wide(zmid[x]) + wide(zx_in[0]) + wide(zx_in[1]) + wide(zx_in[2])).astype(BF)
    arrived(zs)
    block[xrows] = (mine + wide(iz_in[0]) + wide(iz_in[1]) + wide(iz_in[2])).astype(BF)
    ys = [net.send(rows_of(block, at.yo(k)), y_in.at[k - 1], at.to_y(k)) for k in range(1, NY)]
    for d in Z_ORDER:
        wz[d - 1].wait_recv()
        piece = weight_out.at[at.zo(-d), x, c]
        wgather.append([net.send(piece, piece, at.to_x(k)) for k in X_ORDER])
    arrived(ys)
    isum = wide(rows_of(block, y)[...])
    for k in range(NY - 1):
        isum = isum + wide(y_in[k])
    y_sum[...] = isum
    ih = net.send(y_sum, h_in, at.to_half())

    swaps = []
    for d in range(NZ):
        arrived(wgather[d])
        row = weight_out.at[at.zo(-d), :, c]
        swaps.append(net.send(row, row, at.to_core()))
    ih.wait_recv()
    rows_of(item_out, y)[...] = (y_sum[...] + h_in[...]).astype(BF)
    yg = [net.send(rows_of(item_out, y), rows_of(item_out, y), at.to_y(k)) for k in range(1, NY)]
    arrived(swaps)
    arrived(yg)
    net.drain()


VM = pl.BlockSpec(memory_space=pltpu.VMEM)
HB = pl.BlockSpec(memory_space=pltpu.HBM)
LIMIT = 28 * 1024 * 1024


def shape(*dims, dtype=BF):
    return jax.ShapeDtypeStruct(dims, dtype)


def vmem(*dims, dtype=BF):
    return pltpu.VMEM(dims, dtype)


def sems(copies):
    return [pltpu.SemaphoreType.DMA((copies,)), pltpu.SemaphoreType.DMA((copies,))]


def remote(collective_id):
    return pltpu.CompilerParams(
        collective_id=collective_id, has_side_effects=True, vmem_limit_bytes=LIMIT
    )


def per_device(item_features, level_weights, tile_values, tile_order, tile_counts, cotangent):
    tiles = tile_values[0, 0]
    weights = level_weights.reshape(LEVELS * D, H)
    wide_row = (SHARE, LEVELS * D)
    hidden, item_sum, weight_sum = pl.pallas_call(
        exchange_kernel,
        out_shape=(shape(SHARE, H), shape(TILE, D), shape(NZ, NX, NC, WROWS, TILE)),
        in_specs=[HB] * 6,
        out_specs=(VM, VM, VM),
        scratch_shapes=[
            pltpu.SMEM((1, tile_order.shape[1]), jnp.int32),
            pltpu.SMEM((1, tile_counts.shape[1]), jnp.int32),
            pltpu.SMEM((META,), jnp.int32),
            vmem(LEVELS * D, H),
            vmem(SHARE, H),
            vmem(CAP, TILE, TILE),
            vmem(NZ, NX, NC, TILE, D),
            vmem(CAP, TILE, TILE),
            vmem(NZ, NX, *wide_row),
            vmem(NZ, NX, *wide_row),
            vmem(NZ, NX, *wide_row),
            vmem(NX - 1, NZ, SHARE, LANES_X),
            vmem(NZ, SHARE, LANES_X),
            vmem(NZ - 1, SHARE, LANES_X),
            vmem(NZ - 1, NX, SHARE, LEVELS * D - LANES_X),
            vmem(NX, SHARE, LEVELS * D - LANES_X),
            vmem(NX - 1, SHARE, LEVELS * D - LANES_X),
            vmem(NZ, NX, NC, SHARE, H),
            vmem(NZ, *wide_row),
            vmem(LEVELS * UBLK, TILE, D),
            vmem(CAP + 1, TILE, D, dtype=F32),
            vmem(NX, NC, WROWS, TILE),
            vmem(NX, WROWS, TILE),
            vmem(NX, WROWS, TILE),
            vmem(NX - 1, WROWS, TILE),
            vmem(TILE, TILE),
            vmem(NY - 1, CHUNK, TILE),
            vmem(CHUNK, TILE, dtype=F32),
            vmem(CHUNK, TILE, dtype=F32),
            vmem(TILE, TILE),
            vmem(NZ, NX, TILE, D),
            vmem(NZ, NX, TILE, D),
            vmem(NZ, NX, TILE, D),
            vmem(NX - 1, NZ, ROWS_X, D),
            vmem(NZ, ROWS_X, D),
            vmem(NZ - 1, ROWS_X, D),
            vmem(NZ - 1, NX, ROWS_Z, D),
            vmem(NX, ROWS_Z, D),
            vmem(NX - 1, ROWS_Z, D),
            vmem(TILE, D),
            vmem(NY - 1, CHUNK, D),
            vmem(CHUNK, D, dtype=F32),
            vmem(CHUNK, D, dtype=F32),
        ]
        + [pltpu.SemaphoreType.DMA((6,))]
        + sems(192),
        compiler_params=remote(0),
    )(
        *(
            pltpu.with_memory_space_constraint(array, pltpu.HBM)
            for array in (item_features, weights, cotangent, tiles, tile_order, tile_counts)
        )
    )
    hidden, item_grad, weight_grad = pl.pallas_call(
        finish_kernel,
        out_shape=(shape(SHARE, H), shape(TILE, D, dtype=F32), shape(LEVELS * D, H, dtype=F32)),
        in_specs=[VM] * 3,
        out_specs=(VM,) * 3,
        compiler_params=pltpu.CompilerParams(vmem_limit_bytes=LIMIT),
    )(hidden, item_sum, weight_sum.reshape(NZ, LEVELS * D, TILE))
    return (hidden, item_grad, weight_grad.reshape(LEVELS, D, H))


def solution(mesh):
    in_specs = (
        P("item", None),
        P(),
        P("user", "item", None, None, None),
        P("user", None),
        P("user", None),
        P(("user", "item"), None),
    )
    out_specs = (P(("user", "item"), None), P("item", None), P())
    return jax.shard_map(
        per_device, mesh=mesh, in_specs=in_specs, out_specs=out_specs, check_vma=False
    )
```

```python
import functools

import jax
import jax.numpy as jnp
from jax import lax
from jax.experimental import pallas as pl
from jax.experimental.pallas import tpu as pltpu
from jax.sharding import PartitionSpec as P

MESH = pl.DeviceIdType.MESH
BF = jnp.bfloat16
F32 = jnp.float32
NX, NZ, NC, NY, NH = 4, 4, 2, 8, 2
TILE, D, H, LEVELS, UBLK, CAP = 128, 256, 512, 3, 4, 24
BLOCKS = NX * NZ * NC
SHARE = UBLK * TILE // BLOCKS
WROWS = LEVELS * D // (NX * NC)


class Place:
    def __init__(self):
        item = lax.axis_index("item")
        user = lax.axis_index("user")
        self.c = lax.rem(item, NC)
        self.x = lax.rem(lax.div(item, NC), NX)
        self.zl = lax.div(item, NC * NX)
        self.y = lax.rem(user, NY)
        self.zh = lax.div(user, NY)

    def dev(self, zh=None, y=None, zl=None, x=None, c=None):
        pick = lambda value, own: own if value is None else value
        user = pick(zh, self.zh) * NY + pick(y, self.y)
        item = (pick(zl, self.zl) * NX + pick(x, self.x)) * NC + pick(c, self.c)
        return (user, item)

    def xo(self, k):
        return lax.rem(self.x + (k + NX), NX)

    def zo(self, k):
        return lax.rem(self.zl + (k + NZ), NZ)

    def yo(self, k):
        return lax.rem(self.y + (k + NY), NY)

    def to_x(self, k):
        return self.dev(x=self.xo(k))

    def to_z(self, k):
        return self.dev(zl=self.zo(k))

    def to_z8(self, k):
        z = lax.rem(self.zh * NZ + self.zl + (k + NZ * NH), NZ * NH)
        return self.dev(zh=lax.div(z, NZ), zl=lax.rem(z, NZ))

    def to_y(self, k):
        return self.dev(y=self.yo(k))

    def to_core(self):
        return self.dev(c=1 - self.c)

    def to_half(self):
        return self.dev(zh=1 - self.zh)


class Net:
    def __init__(self, send_sems, recv_sems):
        self.send_sems, self.recv_sems, self.copies = send_sems, recv_sems, []

    def send(self, src, dst, device):
        at = len(self.copies)
        copy = pltpu.make_async_remote_copy(
            src_ref=src,
            dst_ref=dst,
            send_sem=self.send_sems.at[at],
            recv_sem=self.recv_sems.at[at],
            device_id=device,
            device_id_type=MESH,
        )
        copy.start()
        self.copies.append(copy)
        return copy

    def drain(self):
        for copy in self.copies:
            copy.wait_send()


def greet(devices):
    barrier = pltpu.get_barrier_semaphore()
    for device in devices:
        pl.semaphore_signal(barrier, inc=1, device_id=device, device_id_type=MESH)
    pl.semaphore_wait(barrier, len(devices))


def wide(value):
    return value.astype(F32)


def finish_kernel(hidden_ref, item_ref, weight_ref, hidden_out, item_out, weight_out):
    hidden_out[...] = hidden_ref[...]
    item_out[...] = wide(item_ref[...])
    scale = 1.0 / (NH * NY * UBLK * TILE) ** 0.5
    for z in range(NZ):
        weight_out[:, z * TILE : (z + 1) * TILE] = wide(weight_ref[z]) * scale


NONE = CAP
BLK, TGT, PREV_BLK, PREV_TGT, LAST_BLK = (CAP * i for i in range(5))
LAST_TGT = LAST_BLK + BLOCKS
META = LAST_TGT + LEVELS * UBLK
ROWS_X = 80
FEAT_Z = 64
LANES_X = 512
ROWS_Z = TILE - ROWS_X
CHUNK = TILE // NY
X_ORDER = (2, 1, -1)
Z_ORDER = (1, 2, 3)


def tile_lists(order, counts, meta):
    item = lax.axis_index("item")
    before = jnp.int32(0)
    for i in range(BLOCKS):
        before = before + jnp.where(i < item, counts[0, i], 0)
    holding = counts[0, item]
    blocks, targets = [], []
    for t in range(CAP):
        slot = order[0, jnp.minimum(before + t, order.shape[1] - 1)]
        live = t < holding
        blocks.append(jnp.where(live, lax.rem(slot, BLOCKS), -1))
        targets.append(jnp.where(live, lax.div(slot, BLOCKS), -1))
        meta[BLK + t] = jnp.maximum(blocks[t], 0)
        meta[TGT + t] = jnp.maximum(targets[t], 0)
    return blocks, targets


def chain(keys, meta, prev, last, number):
    for t in range(CAP):
        found = jnp.int32(NONE)
        for earlier in range(t):
            found = lax.select(keys[earlier] == keys[t], jnp.int32(earlier), found)
        meta[prev + t] = found

    def step(key, carry):
        found = jnp.int32(NONE)
        for t in range(CAP):
            found = lax.select(keys[t] == key, jnp.int32(t), found)
        meta[last + key] = found
        return carry

    lax.fori_loop(0, number, step, 0)


def exchange_kernel(
    feat_ref,
    weights_hbm,
    cot_hbm,
    tiles_hbm,
    order_hbm,
    counts_hbm,
    hidden_ref,
    item_out,
    weight_out,
    order,
    counts,
    meta_ref,
    weights_ref,
    cot_ref,
    tiles_ref,
    feats,
    turned,
    asrc,
    core_in,
    part,
    x_in,
    mid,
    z_in,
    az_in,
    amid,
    ax_in,
    slopes,
    rows,
    back,
    accs,
    wsrc,
    wcore_in,
    wpart,
    wx_in,
    wblock,
    wy_in,
    wy_sum,
    wh_in,
    wslice,
    isrc,
    icore_in,
    ipart,
    ix_in,
    imid,
    iz_in,
    zz_in,
    zmid,
    zx_in,
    block,
    y_in,
    y_sum,
    h_in,
    local_sems,
    send_sems,
    recv_sems,
):
    at = Place()
    net = Net(send_sems, recv_sems)
    zl, x, c, y = at.zl, at.x, at.c, at.y

    def arrived(copies):
        for copy in copies:
            copy.wait_recv()

    def rows_of(ref, at_y):
        return ref.at[pl.ds(pl.multiple_of(at_y * CHUNK, CHUNK), CHUNK)]

    loads = [
        pltpu.make_async_copy(src, dst, local_sems.at[i])
        for i, (src, dst) in enumerate(
            (
                (order_hbm, order),
                (counts_hbm, counts),
                (feat_ref, feats.at[zl, x, c]),
                (tiles_hbm, tiles_ref),
                (weights_hbm, weights_ref),
                (cot_hbm, cot_ref),
            )
        )
    ]
    for load in loads:
        load.start()
    greet(
        [at.to_core()]
        + [at.to_x(k) for k in X_ORDER]
        + [at.to_z8(k) for k in range(1, NZ * NH)]
        + [at.to_y(k) for k in range(1, NY)]
    )

    first_rows, other_rows = (0, 32, FEAT_Z), (FEAT_Z, FEAT_Z + 32, TILE)

    def send_rows(z, xx, first, last, device, own):
        there = feats.at[z, xx, c, first:last]
        return net.send(feat_ref.at[first:last] if own else there, there, device)

    def z_sends(xx, cut, own):
        low, middle, high = cut
        return (
            send_rows(zl, xx, low, high, at.to_z8(1), own),
            send_rows(zl, xx, low, high, at.to_z8(-1), own),
            send_rows(zl, xx, low, middle, at.to_z8(2), own),
            send_rows(zl, xx, middle, high, at.to_z8(-2), own),
        )

    def x_sends(z, first, last, own):
        return {-k: send_rows(z, x, first, last, at.to_x(k), own) for k in (1, -1, 2)}

    z_first = z_sends(x, first_rows, True)
    x_first = x_sends(zl, FEAT_Z, TILE, True)
    x_of = {0: x_sends(zl, 0, FEAT_Z, True)}
    z_of = {0: z_sends(x, other_rows, True)}
    loads[0].wait()
    loads[1].wait()
    blocks, targets = tile_lists(order, counts, meta_ref)
    x_first[-1].wait_recv()
    z_of[-1] = z_sends(at.xo(-1), other_rows, False)
    z_first[0].wait_recv()
    x_of[-1] = x_sends(at.zo(-1), 0, FEAT_Z, False)
    x_first[1].wait_recv()
    z_of[1] = z_sends(at.xo(1), other_rows, False)
    z_first[1].wait_recv()
    x_of[1] = x_sends(at.zo(1), 0, FEAT_Z, False)
    x_first[-2].wait_recv()
    z_of[2] = z_sends(at.xo(2), other_rows, False)
    arrived(z_first[2:])
    x_of[2] = x_sends(at.zo(2), 0, FEAT_Z, False)
    loads[3].wait()
    for t in range(CAP):
        turned[t] = tiles_ref[t].T
    chain(targets, meta_ref, PREV_TGT, LAST_TGT, LEVELS * UBLK)
    accs[NONE] = jnp.zeros((TILE, D), F32)
    swaps = []
    loads[2].wait()
    for d in (0, -1, 1, 2):
        arrived(z_of[d])
        row = feats.at[:, at.xo(d), c, FEAT_Z:]
        swaps.append(net.send(row, row, at.to_core()))
    for d in (0, -1, 1, 2):
        arrived(x_of[d].values())
        row = feats.at[at.zo(d), :, c, :FEAT_Z]
        swaps.append(net.send(row, row, at.to_core()))
    arrived(swaps)

    for t in range(CAP):
        b = meta_ref[BLK + t]
        accs[t] = (
            jnp.dot(
                tiles_ref[t],
                feats[lax.div(b, NX * NC), lax.rem(lax.div(b, NC), NX), lax.rem(b, NC)],
                preferred_element_type=F32,
            )
            + accs[meta_ref[PREV_TGT + t]]
        )

    def agg_of(z, level, xx, cc):
        first = pl.multiple_of((xx * NC + cc) * SHARE, SHARE)
        return accs[meta_ref[LAST_TGT + level * UBLK + z], pl.ds(first, SHARE), :]

    core = []
    for k in X_ORDER + (0,):
        xx = at.xo(k)
        for z in range(NZ):
            for level in range(LEVELS):
                asrc[z, xx, :, level * D : (level + 1) * D] = agg_of(z, level, xx, 1 - c).astype(BF)
        core.append((k, net.send(asrc.at[:, xx], core_in.at[:, xx], at.to_core())))
    xlanes, zlanes = slice(0, LANES_X), slice(LANES_X, LEVELS * D)
    x_copies = []
    for k, copy in core:
        copy.wait_recv()
        xx = at.xo(k)
        for z in range(NZ):
            for level in range(LEVELS):
                lanes = slice(level * D, (level + 1) * D)
                part[z, xx, :, lanes] = (
                    agg_of(z, level, xx, c) + wide(core_in[z, xx, :, lanes])
                ).astype(BF)
        if k:
            x_copies.append(
                net.send(part.at[:, xx, :, xlanes], x_in.at[len(x_copies)], at.to_x(k))
            )
    az = [net.send(part.at[at.zo(k), :, :, zlanes], az_in.at[k - 1], at.to_z(k)) for k in Z_ORDER]
    chain(blocks, meta_ref, PREV_BLK, LAST_BLK, BLOCKS)
    loads[4].wait()
    loads[5].wait()
    arrived(x_copies)

    def x_total(index):
        total = wide(part[index, x, :, xlanes])
        for j in range(NX - 1):
            total = total + wide(x_in[j, index])
        return total

    z_copies = []
    for k in Z_ORDER:
        mid[at.zo(k)] = x_total(at.zo(k)).astype(BF)
        z_copies.append(net.send(mid.at[at.zo(k)], z_in.at[k - 1], at.to_z(k)))
    left = x_total(zl)
    arrived(az)

    def z_total(index):
        total = wide(part[zl, index, :, zlanes])
        for j in range(NZ - 1):
            total = total + wide(az_in[j, index])
        return total

    ax = []
    for j, k in enumerate(X_ORDER):
        amid[at.xo(k)] = z_total(at.xo(k)).astype(BF)
        ax.append(net.send(amid.at[at.xo(k)], ax_in.at[j], at.to_x(k)))
    right = z_total(x)
    arrived(ax)
    for j in range(NX - 1):
        right = right + wide(ax_in[j])
    arrived(z_copies)
    for j in range(NZ - 1):
        left = left + wide(z_in[j])
    total = jnp.concatenate([left, right], axis=1)

    upper = total.astype(BF)
    lower = (total - wide(upper)).astype(BF)
    both = jnp.dot(
        jnp.concatenate([upper, lower], axis=0), weights_ref[...], preferred_element_type=F32
    )
    pre = both[:SHARE] + both[SHARE:]
    sig = 1.0 / (1.0 + jnp.exp(-pre))
    hidden_ref[...] = (pre * sig).astype(BF)
    slopes[zl, x, c] = (wide(cot_ref[...]) * (sig * (1.0 + pre * (1.0 - sig)))).astype(BF)
    rows[zl] = upper

    own = slopes.at[zl, x, c]
    to_z = [net.send(own, own, at.to_z(k)) for k in Z_ORDER]
    to_x = [[net.send(own, own, at.to_x(k)) for k in X_ORDER]]
    row_copies = [net.send(rows.at[zl], rows.at[zl], at.to_z(k)) for k in Z_ORDER]
    for d in Z_ORDER:
        to_z[d - 1].wait_recv()
        piece = slopes.at[at.zo(-d), x, c]
        to_x.append([net.send(piece, piece, at.to_x(k)) for k in X_ORDER])
    arrived(row_copies)
    column = pl.ds(pl.multiple_of(zl * TILE, TILE), TILE)
    mine = jnp.concatenate([slopes[z, x, c, :, column] for z in range(NZ)], axis=0)
    wsrc[...] = (
        lax.dot_general(
            rows[...].reshape(NZ * SHARE, LEVELS * D),
            mine,
            (((0,), (0,)), ((), ())),
            preferred_element_type=F32,
        )
        .astype(BF)
        .reshape(NX, NC, WROWS, TILE)
    )
    wcore = net.send(wsrc.at[:, 1 - c], wcore_in, at.to_core())
    swaps = []
    for d in range(NZ):
        arrived(to_x[d])
        row = slopes.at[at.zo(-d), :, c]
        swaps.append(net.send(row, row, at.to_core()))

    wcore.wait_recv()
    wpart[...] = (wide(wsrc[:, c]) + wide(wcore_in[...])).astype(BF)
    wx = [net.send(wpart.at[at.xo(k)], wx_in.at[j], at.to_x(k)) for j, k in enumerate(X_ORDER)]

    for d in range(NZ):
        swaps[d].wait_recv()
        z = at.zo(-d)
        mine = slopes[z].reshape(TILE, H)
        for level in range(LEVELS):
            back[level * UBLK + z] = lax.dot_general(
                mine,
                weights_ref[level * D : (level + 1) * D],
                (((1,), (1,)), ((), ())),
                preferred_element_type=F32,
            ).astype(BF)

    for t in range(CAP):
        accs[t] = (
            jnp.dot(turned[t], back[meta_ref[TGT + t]], preferred_element_type=F32)
            + accs[meta_ref[PREV_BLK + t]]
        )

    def grads_of(z, xx, cc):
        return accs[meta_ref[LAST_BLK + (z * NX + xx) * NC + cc]]

    core = []
    for k in X_ORDER + (0,):
        xx = at.xo(k)
        for z in range(NZ):
            isrc[z, xx] = grads_of(z, xx, 1 - c).astype(BF)
        core.append((k, net.send(isrc.at[:, xx], icore_in.at[:, xx], at.to_core())))

    arrived(wx)
    wblock[:WROWS] = (wide(wpart[x]) + wide(wx_in[0]) + wide(wx_in[1]) + wide(wx_in[2])).astype(BF)
    wblock[WROWS:] = jnp.zeros((TILE - WROWS, TILE), BF)
    wy = [net.send(rows_of(wblock, at.yo(k)), wy_in.at[k - 1], at.to_y(k)) for k in range(1, NY)]

    xrows, zrows = slice(0, ROWS_X), slice(ROWS_X, TILE)
    x_copies = []
    for k, copy in core:
        copy.wait_recv()
        xx = at.xo(k)
        for z in range(NZ):
            ipart[z, xx] = (grads_of(z, xx, c) + wide(icore_in[z, xx])).astype(BF)
        if k:
            x_copies.append(net.send(ipart.at[:, xx, xrows], ix_in.at[len(x_copies)], at.to_x(k)))
    zz = [net.send(ipart.at[at.zo(k), :, zrows], zz_in.at[k - 1], at.to_z(k)) for k in Z_ORDER]

    arrived(wy)
    wsum = wide(rows_of(wblock, y)[...])
    for k in range(NY - 1):
        wsum = wsum + wide(wy_in[k])
    wy_sum[...] = wsum
    wh = net.send(wy_sum, wh_in, at.to_half())

    arrived(zz)
    zmid[...] = (
        wide(ipart[zl, :, zrows]) + wide(zz_in[0]) + wide(zz_in[1]) + wide(zz_in[2])
    ).astype(BF)
    zx = [net.send(zmid.at[at.xo(k)], zx_in.at[j], at.to_x(k)) for j, k in enumerate(X_ORDER)]

    wh.wait_recv()
    rows_of(wslice, y)[...] = (wy_sum[...] + wh_in[...]).astype(BF)
    wyg = [net.send(rows_of(wslice, y), rows_of(wslice, y), at.to_y(k)) for k in range(1, NY)]

    arrived(x_copies)

    def ix_total(index):
        total = wide(ipart[index, x, xrows])
        for j in range(NX - 1):
            total = total + wide(ix_in[j, index])
        return total

    zs = []
    for k in Z_ORDER:
        z = at.zo(k)
        imid[z] = ix_total(z).astype(BF)
        zs.append(net.send(imid.at[z], iz_in.at[k - 1], at.to_z(k)))
    mine = ix_total(zl)

    arrived(wyg)
    weight_out[zl, x, c] = wslice[:WROWS]
    own = weight_out.at[zl, x, c]
    wz = [net.send(own, own, at.to_z(k)) for k in Z_ORDER]
    wgather = [[net.send(own, own, at.to_x(k)) for k in X_ORDER]]

    arrived(zx)
    block[zrows] = (wide(zmid[x]) + wide(zx_in[0]) + wide(zx_in[1]) + wide(zx_in[2])).astype(BF)
    arrived(zs)
    block[xrows] = (mine + wide(iz_in[0]) + wide(iz_in[1]) + wide(iz_in[2])).astype(BF)
    ys = [net.send(rows_of(block, at.yo(k)), y_in.at[k - 1], at.to_y(k)) for k in range(1, NY)]
    for d in Z_ORDER:
        wz[d - 1].wait_recv()
        piece = weight_out.at[at.zo(-d), x, c]
        wgather.append([net.send(piece, piece, at.to_x(k)) for k in X_ORDER])
    arrived(ys)
    isum = wide(rows_of(block, y)[...])
    for k in range(NY - 1):
        isum = isum + wide(y_in[k])
    y_sum[...] = isum
    ih = net.send(y_sum, h_in, at.to_half())

    swaps = []
    for d in range(NZ):
        arrived(wgather[d])
        row = weight_out.at[at.zo(-d), :, c]
        swaps.append(net.send(row, row, at.to_core()))
    ih.wait_recv()
    rows_of(item_out, y)[...] = (y_sum[...] + h_in[...]).astype(BF)
    yg = [net.send(rows_of(item_out, y), rows_of(item_out, y), at.to_y(k)) for k in range(1, NY)]
    arrived(swaps)
    arrived(yg)
    net.drain()


VM = pl.BlockSpec(memory_space=pltpu.VMEM)
HB = pl.BlockSpec(memory_space=pltpu.HBM)
LIMIT = 28 * 1024 * 1024


def shape(*dims, dtype=BF):
    return jax.ShapeDtypeStruct(dims, dtype)


def vmem(*dims, dtype=BF):
    return pltpu.VMEM(dims, dtype)


def sems(copies):
    return [pltpu.SemaphoreType.DMA((copies,)), pltpu.SemaphoreType.DMA((copies,))]


def remote(collective_id):
    return pltpu.CompilerParams(
        collective_id=collective_id, has_side_effects=True, vmem_limit_bytes=LIMIT
    )


def per_device(item_features, level_weights, tile_values, tile_order, tile_counts, cotangent):
    tiles = tile_values[0, 0]
    weights = level_weights.reshape(LEVELS * D, H)
    wide_row = (SHARE, LEVELS * D)
    hidden, item_sum, weight_sum = pl.pallas_call(
        exchange_kernel,
        out_shape=(shape(SHARE, H), shape(TILE, D), shape(NZ, NX, NC, WROWS, TILE)),
        in_specs=[HB] * 6,
        out_specs=(VM, VM, VM),
        scratch_shapes=[
            pltpu.SMEM((1, tile_order.shape[1]), jnp.int32),
            pltpu.SMEM((1, tile_counts.shape[1]), jnp.int32),
            pltpu.SMEM((META,), jnp.int32),
            vmem(LEVELS * D, H),
            vmem(SHARE, H),
            vmem(CAP, TILE, TILE),
            vmem(NZ, NX, NC, TILE, D),
            vmem(CAP, TILE, TILE),
            vmem(NZ, NX, *wide_row),
            vmem(NZ, NX, *wide_row),
            vmem(NZ, NX, *wide_row),
            vmem(NX - 1, NZ, SHARE, LANES_X),
            vmem(NZ, SHARE, LANES_X),
            vmem(NZ - 1, SHARE, LANES_X),
            vmem(NZ - 1, NX, SHARE, LEVELS * D - LANES_X),
            vmem(NX, SHARE, LEVELS * D - LANES_X),
            vmem(NX - 1, SHARE, LEVELS * D - LANES_X),
            vmem(NZ, NX, NC, SHARE, H),
            vmem(NZ, *wide_row),
            vmem(LEVELS * UBLK, TILE, D),
            vmem(CAP + 1, TILE, D, dtype=F32),
            vmem(NX, NC, WROWS, TILE),
            vmem(NX, WROWS, TILE),
            vmem(NX, WROWS, TILE),
            vmem(NX - 1, WROWS, TILE),
            vmem(TILE, TILE),
            vmem(NY - 1, CHUNK, TILE),
            vmem(CHUNK, TILE, dtype=F32),
            vmem(CHUNK, TILE, dtype=F32),
            vmem(TILE, TILE),
            vmem(NZ, NX, TILE, D),
            vmem(NZ, NX, TILE, D),
            vmem(NZ, NX, TILE, D),
            vmem(NX - 1, NZ, ROWS_X, D),
            vmem(NZ, ROWS_X, D),
            vmem(NZ - 1, ROWS_X, D),
            vmem(NZ - 1, NX, ROWS_Z, D),
            vmem(NX, ROWS_Z, D),
            vmem(NX - 1, ROWS_Z, D),
            vmem(TILE, D),
            vmem(NY - 1, CHUNK, D),
            vmem(CHUNK, D, dtype=F32),
            vmem(CHUNK, D, dtype=F32),
        ]
        + [pltpu.SemaphoreType.DMA((6,))]
        + sems(192),
        compiler_params=remote(0),
    )(
        *(
            pltpu.with_memory_space_constraint(array, pltpu.HBM)
            for array in (item_features, weights, cotangent, tiles, tile_order, tile_counts)
        )
    )
    hidden, item_grad, weight_grad = pl.pallas_call(
        finish_kernel,
        out_shape=(shape(SHARE, H), shape(TILE, D, dtype=F32), shape(LEVELS * D, H, dtype=F32)),
        in_specs=[VM] * 3,
        out_specs=(VM,) * 3,
        compiler_params=pltpu.CompilerParams(vmem_limit_bytes=LIMIT),
    )(hidden, item_sum, weight_sum.reshape(NZ, LEVELS * D, TILE))
    return (hidden, item_grad, weight_grad.reshape(LEVELS, D, H))


def solution(mesh):
    in_specs = (
        P("item", None),
        P(),
        P("user", "item", None, None, None),
        P("user", None),
        P("user", None),
        P(("user", "item"), None),
    )
    out_specs = (P(("user", "item"), None), P("item", None), P())
    return jax.shard_map(
        per_device, mesh=mesh, in_specs=in_specs, out_specs=out_specs, check_vma=False
    )
```

```python
import functools

import jax
import jax.numpy as jnp
from jax import lax
from jax.experimental import pallas as pl
from jax.experimental.pallas import tpu as pltpu
from jax.sharding import PartitionSpec as P

MESH = pl.DeviceIdType.MESH
BF = jnp.bfloat16
F32 = jnp.float32
NX, NZ, NC, NY, NH = 4, 4, 2, 8, 2
TILE, D, H, LEVELS, UBLK, CAP = 128, 256, 512, 3, 4, 24
BLOCKS = NX * NZ * NC
SHARE = UBLK * TILE // BLOCKS
WROWS = LEVELS * D // (NX * NC)


class Place:
    def __init__(self):
        item = lax.axis_index("item")
        user = lax.axis_index("user")
        self.c = lax.rem(item, NC)
        self.x = lax.rem(lax.div(item, NC), NX)
        self.zl = lax.div(item, NC * NX)
        self.y = lax.rem(user, NY)
        self.zh = lax.div(user, NY)

    def dev(self, zh=None, y=None, zl=None, x=None, c=None):
        pick = lambda value, own: own if value is None else value
        user = pick(zh, self.zh) * NY + pick(y, self.y)
        item = (pick(zl, self.zl) * NX + pick(x, self.x)) * NC + pick(c, self.c)
        return (user, item)

    def xo(self, k):
        return lax.rem(self.x + (k + NX), NX)

    def zo(self, k):
        return lax.rem(self.zl + (k + NZ), NZ)

    def yo(self, k):
        return lax.rem(self.y + (k + NY), NY)

    def to_x(self, k):
        return self.dev(x=self.xo(k))

    def to_z(self, k):
        return self.dev(zl=self.zo(k))

    def to_z8(self, k):
        z = lax.rem(self.zh * NZ + self.zl + (k + NZ * NH), NZ * NH)
        return self.dev(zh=lax.div(z, NZ), zl=lax.rem(z, NZ))

    def to_y(self, k):
        return self.dev(y=self.yo(k))

    def to_core(self):
        return self.dev(c=1 - self.c)

    def to_half(self):
        return self.dev(zh=1 - self.zh)


class Net:
    def __init__(self, send_sems, recv_sems):
        self.send_sems, self.recv_sems, self.copies = send_sems, recv_sems, []

    def send(self, src, dst, device):
        at = len(self.copies)
        copy = pltpu.make_async_remote_copy(
            src_ref=src,
            dst_ref=dst,
            send_sem=self.send_sems.at[at],
            recv_sem=self.recv_sems.at[at],
            device_id=device,
            device_id_type=MESH,
        )
        copy.start()
        self.copies.append(copy)
        return copy

    def drain(self):
        for copy in self.copies:
            copy.wait_send()


def greet(devices):
    barrier = pltpu.get_barrier_semaphore()
    for device in devices:
        pl.semaphore_signal(barrier, inc=1, device_id=device, device_id_type=MESH)
    return lambda: pl.semaphore_wait(barrier, len(devices))


def wide(value):
    return value.astype(F32)


def finish_kernel(hidden_ref, item_ref, weight_ref, hidden_out, item_out, weight_out):
    hidden_out[...] = hidden_ref[...]
    item_out[...] = wide(item_ref[...])
    scale = 1.0 / (NH * NY * UBLK * TILE) ** 0.5
    for z in range(NZ):
        weight_out[:, z * TILE : (z + 1) * TILE] = wide(weight_ref[z]) * scale


NONE = CAP
BLK, TGT, PREV_BLK, PREV_TGT, LAST_BLK = (CAP * i for i in range(5))
LAST_TGT = LAST_BLK + BLOCKS
META = LAST_TGT + LEVELS * UBLK
ROWS_X = 80
FEAT_Z = 64
LANES_X = 512
ROWS_Z = TILE - ROWS_X
CHUNK = TILE // NY
X_ORDER = (2, 1, -1)
Z_ORDER = (1, 2, 3)
Y_ORDER = (4, 3, 5, 2, 6, 1, 7)


def tile_lists(order, counts, meta):
    item = lax.axis_index("item")
    before = jnp.int32(0)
    for i in range(BLOCKS):
        before = before + jnp.where(i < item, counts[0, i], 0)
    holding = counts[0, item]
    blocks, targets = [], []
    for t in range(CAP):
        slot = order[0, jnp.minimum(before + t, order.shape[1] - 1)]
        live = t < holding
        blocks.append(jnp.where(live, lax.rem(slot, BLOCKS), -1))
        targets.append(jnp.where(live, lax.div(slot, BLOCKS), -1))
        meta[BLK + t] = jnp.maximum(blocks[t], 0)
        meta[TGT + t] = jnp.maximum(targets[t], 0)
    return blocks, targets


def chain(keys, meta, prev, last, number):
    for t in range(CAP):
        found = jnp.int32(NONE)
        for earlier in range(t):
            found = lax.select(keys[earlier] == keys[t], jnp.int32(earlier), found)
        meta[prev + t] = found

    def step(key, carry):
        found = jnp.int32(NONE)
        for t in range(CAP):
            found = lax.select(keys[t] == key, jnp.int32(t), found)
        meta[last + key] = found
        return carry

    lax.fori_loop(0, number, step, 0)


def exchange_kernel(
    feat_ref,
    weights_hbm,
    cot_hbm,
    tiles_hbm,
    order_hbm,
    counts_hbm,
    hidden_ref,
    item_out,
    weight_out,
    order,
    counts,
    meta_ref,
    weights_ref,
    cot_ref,
    tiles_ref,
    feats,
    turned,
    asrc,
    core_in,
    part,
    x_in,
    mid,
    z_in,
    az_in,
    amid,
    ax_in,
    slopes,
    rows,
    back,
    accs,
    wsrc,
    wcore_in,
    wpart,
    wx_in,
    wblock,
    wy_in,
    wy_sum,
    wh_in,
    wslice,
    isrc,
    icore_in,
    ipart,
    ix_in,
    imid,
    iz_in,
    zz_in,
    zmid,
    zx_in,
    block,
    y_in,
    y_sum,
    h_in,
    local_sems,
    send_sems,
    recv_sems,
):
    at = Place()
    net = Net(send_sems, recv_sems)
    zl, x, c, y = at.zl, at.x, at.c, at.y

    def arrived(copies):
        for copy in copies:
            copy.wait_recv()

    def rows_of(ref, at_y):
        return ref.at[pl.ds(pl.multiple_of(at_y * CHUNK, CHUNK), CHUNK)]

    loads = [
        pltpu.make_async_copy(src, dst, local_sems.at[i])
        for i, (src, dst) in enumerate(
            (
                (order_hbm, order),
                (counts_hbm, counts),
                (feat_ref, feats.at[zl, x, c]),
                (tiles_hbm, tiles_ref),
                (weights_hbm, weights_ref),
                (cot_hbm, cot_ref),
            )
        )
    ]
    meet = greet(
        [at.to_core()]
        + [at.to_x(k) for k in X_ORDER]
        + [at.to_z8(k) for k in range(1, NZ * NH)]
        + [at.to_y(k) for k in range(1, NY)]
    )
    for load in loads:
        load.start()
    meet()

    first_rows, other_rows = (0, 32, FEAT_Z), (FEAT_Z, FEAT_Z + 32, TILE)

    def send_rows(z, xx, first, last, device, own):
        there = feats.at[z, xx, c, first:last]
        return net.send(feat_ref.at[first:last] if own else there, there, device)

    def z_sends(xx, cut, own):
        low, middle, high = cut
        return (
            send_rows(zl, xx, low, high, at.to_z8(1), own),
            send_rows(zl, xx, low, high, at.to_z8(-1), own),
            send_rows(zl, xx, low, middle, at.to_z8(2), own),
            send_rows(zl, xx, middle, high, at.to_z8(-2), own),
        )

    def x_sends(z, first, last, own):
        return {-k: send_rows(z, x, first, last, at.to_x(k), own) for k in (1, -1, 2)}

    z_first = z_sends(x, first_rows, True)
    x_first = x_sends(zl, FEAT_Z, TILE, True)
    x_of = {0: x_sends(zl, 0, FEAT_Z, True)}
    z_of = {0: z_sends(x, other_rows, True)}
    loads[0].wait()
    loads[1].wait()
    blocks, targets = tile_lists(order, counts, meta_ref)
    x_first[-1].wait_recv()
    z_of[-1] = z_sends(at.xo(-1), other_rows, False)
    z_first[0].wait_recv()
    x_of[-1] = x_sends(at.zo(-1), 0, FEAT_Z, False)
    x_first[1].wait_recv()
    z_of[1] = z_sends(at.xo(1), other_rows, False)
    z_first[1].wait_recv()
    x_of[1] = x_sends(at.zo(1), 0, FEAT_Z, False)
    x_first[-2].wait_recv()
    z_of[2] = z_sends(at.xo(2), other_rows, False)
    arrived(z_first[2:])
    x_of[2] = x_sends(at.zo(2), 0, FEAT_Z, False)
    loads[3].wait()
    for t in range(CAP):
        turned[t] = tiles_ref[t].T
    chain(targets, meta_ref, PREV_TGT, LAST_TGT, LEVELS * UBLK)
    accs[NONE] = jnp.zeros((TILE, D), F32)
    swaps = []
    loads[2].wait()
    for d in (0, -1, 1, 2):
        arrived(z_of[d])
        row = feats.at[:, at.xo(d), c, FEAT_Z:]
        swaps.append(net.send(row, row, at.to_core()))
    for d in (0, -1, 1, 2):
        arrived(x_of[d].values())
        row = feats.at[at.zo(d), :, c, :FEAT_Z]
        swaps.append(net.send(row, row, at.to_core()))
    arrived(swaps)

    for t in range(CAP):
        b = meta_ref[BLK + t]
        accs[t] = (
            jnp.dot(
                tiles_ref[t],
                feats[lax.div(b, NX * NC), lax.rem(lax.div(b, NC), NX), lax.rem(b, NC)],
                preferred_element_type=F32,
            )
            + accs[meta_ref[PREV_TGT + t]]
        )

    def agg_of(z, level, xx, cc):
        first = pl.multiple_of((xx * NC + cc) * SHARE, SHARE)
        return accs[meta_ref[LAST_TGT + level * UBLK + z], pl.ds(first, SHARE), :]

    core = []
    for k in X_ORDER + (0,):
        xx = at.xo(k)
        for z in range(NZ):
            for level in range(LEVELS):
                asrc[z, xx, :, level * D : (level + 1) * D] = agg_of(z, level, xx, 1 - c).astype(BF)
        core.append((k, net.send(asrc.at[:, xx], core_in.at[:, xx], at.to_core())))
    xlanes, zlanes = slice(0, LANES_X), slice(LANES_X, LEVELS * D)
    x_copies, az = [], []
    for k, copy in core:
        copy.wait_recv()
        xx = at.xo(k)
        for z in range(NZ):
            for level in range(LEVELS):
                lanes = slice(level * D, (level + 1) * D)
                part[z, xx, :, lanes] = (
                    agg_of(z, level, xx, c) + wide(core_in[z, xx, :, lanes])
                ).astype(BF)
        if k:
            x_copies.append(
                net.send(part.at[:, xx, :, xlanes], x_in.at[len(x_copies)], at.to_x(k))
            )
        for j in Z_ORDER:
            az.append(
                net.send(part.at[at.zo(j), xx, :, zlanes], az_in.at[j - 1, xx], at.to_z(j))
            )
    chain(blocks, meta_ref, PREV_BLK, LAST_BLK, BLOCKS)
    loads[4].wait()
    loads[5].wait()
    arrived(x_copies)

    def x_total(index):
        total = wide(part[index, x, :, xlanes])
        for j in range(NX - 1):
            total = total + wide(x_in[j, index])
        return total

    z_copies = []
    for k in Z_ORDER:
        mid[at.zo(k)] = x_total(at.zo(k)).astype(BF)
        z_copies.append(net.send(mid.at[at.zo(k)], z_in.at[k - 1], at.to_z(k)))
    left = x_total(zl)
    arrived(az)

    def z_total(index):
        total = wide(part[zl, index, :, zlanes])
        for j in range(NZ - 1):
            total = total + wide(az_in[j, index])
        return total

    ax = []
    for j, k in enumerate(X_ORDER):
        amid[at.xo(k)] = z_total(at.xo(k)).astype(BF)
        ax.append(net.send(amid.at[at.xo(k)], ax_in.at[j], at.to_x(k)))
    right = z_total(x)
    arrived(ax)
    for j in range(NX - 1):
        right = right + wide(ax_in[j])
    arrived(z_copies)
    for j in range(NZ - 1):
        left = left + wide(z_in[j])
    total = jnp.concatenate([left, right], axis=1)

    upper = total.astype(BF)
    lower = (total - wide(upper)).astype(BF)
    both = jnp.dot(
        jnp.concatenate([upper, lower], axis=0), weights_ref[...], preferred_element_type=F32
    )
    pre = both[:SHARE] + both[SHARE:]
    sig = 1.0 / (1.0 + jnp.exp(-pre))
    hidden_ref[...] = (pre * sig).astype(BF)
    slopes[zl, x, c] = (wide(cot_ref[...]) * (sig * (1.0 + pre * (1.0 - sig)))).astype(BF)
    rows[zl] = upper

    own = slopes.at[zl, x, c]
    to_z = [net.send(own, own, at.to_z(k)) for k in Z_ORDER]
    to_x = [[net.send(own, own, at.to_x(k)) for k in X_ORDER]]
    row_copies = [net.send(rows.at[zl], rows.at[zl], at.to_z(k)) for k in Z_ORDER]
    for d in Z_ORDER:
        to_z[d - 1].wait_recv()
        piece = slopes.at[at.zo(-d), x, c]
        to_x.append([net.send(piece, piece, at.to_x(k)) for k in X_ORDER])
    arrived(row_copies)
    column = pl.ds(pl.multiple_of(zl * TILE, TILE), TILE)
    mine = jnp.concatenate([slopes[z, x, c, :, column] for z in range(NZ)], axis=0)
    wsrc[...] = (
        lax.dot_general(
            rows[...].reshape(NZ * SHARE, LEVELS * D),
            mine,
            (((0,), (0,)), ((), ())),
            preferred_element_type=F32,
        )
        .astype(BF)
        .reshape(NX, NC, WROWS, TILE)
    )
    wcore = net.send(wsrc.at[:, 1 - c], wcore_in, at.to_core())
    swaps = []
    for d in range(NZ):
        arrived(to_x[d])
        row = slopes.at[at.zo(-d), :, c]
        swaps.append(net.send(row, row, at.to_core()))

    wcore.wait_recv()
    wpart[...] = (wide(wsrc[:, c]) + wide(wcore_in[...])).astype(BF)
    wx = [net.send(wpart.at[at.xo(k)], wx_in.at[j], at.to_x(k)) for j, k in enumerate(X_ORDER)]

    for d in range(NZ):
        swaps[d].wait_recv()
        z = at.zo(-d)
        mine = slopes[z].reshape(TILE, H)
        for level in range(LEVELS):
            back[level * UBLK + z] = lax.dot_general(
                mine,
                weights_ref[level * D : (level + 1) * D],
                (((1,), (1,)), ((), ())),
                preferred_element_type=F32,
            ).astype(BF)

    for t in range(CAP):
        accs[t] = (
            jnp.dot(turned[t], back[meta_ref[TGT + t]], preferred_element_type=F32)
            + accs[meta_ref[PREV_BLK + t]]
        )

    def grads_of(z, xx, cc):
        return accs[meta_ref[LAST_BLK + (z * NX + xx) * NC + cc]]

    core = []
    for k in X_ORDER + (0,):
        xx = at.xo(k)
        for z in range(NZ):
            isrc[z, xx] = grads_of(z, xx, 1 - c).astype(BF)
        core.append((k, net.send(isrc.at[:, xx], icore_in.at[:, xx], at.to_core())))

    arrived(wx)
    wblock[:WROWS] = (wide(wpart[x]) + wide(wx_in[0]) + wide(wx_in[1]) + wide(wx_in[2])).astype(BF)
    wblock[WROWS:] = jnp.zeros((TILE - WROWS, TILE), BF)
    wy = [net.send(rows_of(wblock, at.yo(k)), wy_in.at[k - 1], at.to_y(k)) for k in Y_ORDER]

    xrows, zrows = slice(0, ROWS_X), slice(ROWS_X, TILE)
    x_copies, zz = [], []
    for k, copy in core:
        copy.wait_recv()
        xx = at.xo(k)
        for z in range(NZ):
            ipart[z, xx] = (grads_of(z, xx, c) + wide(icore_in[z, xx])).astype(BF)
        if k:
            x_copies.append(net.send(ipart.at[:, xx, xrows], ix_in.at[len(x_copies)], at.to_x(k)))
        for j in Z_ORDER:
            zz.append(net.send(ipart.at[at.zo(j), xx, zrows], zz_in.at[j - 1, xx], at.to_z(j)))

    arrived(wy)
    wsum = wide(rows_of(wblock, y)[...])
    for k in range(NY - 1):
        wsum = wsum + wide(wy_in[k])
    wy_sum[...] = wsum
    wh = net.send(wy_sum, wh_in, at.to_half())

    arrived(zz)
    zmid[...] = (
        wide(ipart[zl, :, zrows]) + wide(zz_in[0]) + wide(zz_in[1]) + wide(zz_in[2])
    ).astype(BF)
    zx = [net.send(zmid.at[at.xo(k)], zx_in.at[j], at.to_x(k)) for j, k in enumerate(X_ORDER)]

    wh.wait_recv()
    rows_of(wslice, y)[...] = (wy_sum[...] + wh_in[...]).astype(BF)
    wyg = [net.send(rows_of(wslice, y), rows_of(wslice, y), at.to_y(k)) for k in Y_ORDER]

    arrived(x_copies)

    def ix_total(index):
        total = wide(ipart[index, x, xrows])
        for j in range(NX - 1):
            total = total + wide(ix_in[j, index])
        return total

    zs = []
    for k in Z_ORDER:
        z = at.zo(k)
        imid[z] = ix_total(z).astype(BF)
        zs.append(net.send(imid.at[z], iz_in.at[k - 1], at.to_z(k)))
    mine = ix_total(zl)

    arrived(wyg)
    weight_out[zl, x, c] = wslice[:WROWS]
    own = weight_out.at[zl, x, c]
    wz = [net.send(own, own, at.to_z(k)) for k in Z_ORDER]
    wgather = [[net.send(own, own, at.to_x(k)) for k in X_ORDER]]

    arrived(zx)
    block[zrows] = (wide(zmid[x]) + wide(zx_in[0]) + wide(zx_in[1]) + wide(zx_in[2])).astype(BF)
    arrived(zs)
    block[xrows] = (mine + wide(iz_in[0]) + wide(iz_in[1]) + wide(iz_in[2])).astype(BF)
    ys = [net.send(rows_of(block, at.yo(k)), y_in.at[k - 1], at.to_y(k)) for k in Y_ORDER]
    for d in Z_ORDER:
        wz[d - 1].wait_recv()
        piece = weight_out.at[at.zo(-d), x, c]
        wgather.append([net.send(piece, piece, at.to_x(k)) for k in X_ORDER])
    arrived(ys)
    isum = wide(rows_of(block, y)[...])
    for k in range(NY - 1):
        isum = isum + wide(y_in[k])
    y_sum[...] = isum
    ih = net.send(y_sum, h_in, at.to_half())

    swaps = []
    for d in range(NZ):
        arrived(wgather[d])
        row = weight_out.at[at.zo(-d), :, c]
        swaps.append(net.send(row, row, at.to_core()))
    ih.wait_recv()
    rows_of(item_out, y)[...] = (y_sum[...] + h_in[...]).astype(BF)
    yg = [net.send(rows_of(item_out, y), rows_of(item_out, y), at.to_y(k)) for k in Y_ORDER]
    arrived(swaps)
    arrived(yg)
    net.drain()


VM = pl.BlockSpec(memory_space=pltpu.VMEM)
HB = pl.BlockSpec(memory_space=pltpu.HBM)
LIMIT = 28 * 1024 * 1024


def shape(*dims, dtype=BF):
    return jax.ShapeDtypeStruct(dims, dtype)


def vmem(*dims, dtype=BF):
    return pltpu.VMEM(dims, dtype)


def sems(copies):
    return [pltpu.SemaphoreType.DMA((copies,)), pltpu.SemaphoreType.DMA((copies,))]


def remote(collective_id):
    return pltpu.CompilerParams(
        collective_id=collective_id, has_side_effects=True, vmem_limit_bytes=LIMIT
    )


def per_device(item_features, level_weights, tile_values, tile_order, tile_counts, cotangent):
    tiles = tile_values[0, 0]
    weights = level_weights.reshape(LEVELS * D, H)
    wide_row = (SHARE, LEVELS * D)
    hidden, item_sum, weight_sum = pl.pallas_call(
        exchange_kernel,
        out_shape=(shape(SHARE, H), shape(TILE, D), shape(NZ, NX, NC, WROWS, TILE)),
        in_specs=[HB] * 6,
        out_specs=(VM, VM, VM),
        scratch_shapes=[
            pltpu.SMEM((1, tile_order.shape[1]), jnp.int32),
            pltpu.SMEM((1, tile_counts.shape[1]), jnp.int32),
            pltpu.SMEM((META,), jnp.int32),
            vmem(LEVELS * D, H),
            vmem(SHARE, H),
            vmem(CAP, TILE, TILE),
            vmem(NZ, NX, NC, TILE, D),
            vmem(CAP, TILE, TILE),
            vmem(NZ, NX, *wide_row),
            vmem(NZ, NX, *wide_row),
            vmem(NZ, NX, *wide_row),
            vmem(NX - 1, NZ, SHARE, LANES_X),
            vmem(NZ, SHARE, LANES_X),
            vmem(NZ - 1, SHARE, LANES_X),
            vmem(NZ - 1, NX, SHARE, LEVELS * D - LANES_X),
            vmem(NX, SHARE, LEVELS * D - LANES_X),
            vmem(NX - 1, SHARE, LEVELS * D - LANES_X),
            vmem(NZ, NX, NC, SHARE, H),
            vmem(NZ, *wide_row),
            vmem(LEVELS * UBLK, TILE, D),
            vmem(CAP + 1, TILE, D, dtype=F32),
            vmem(NX, NC, WROWS, TILE),
            vmem(NX, WROWS, TILE),
            vmem(NX, WROWS, TILE),
            vmem(NX - 1, WROWS, TILE),
            vmem(TILE, TILE),
            vmem(NY - 1, CHUNK, TILE),
            vmem(CHUNK, TILE, dtype=F32),
            vmem(CHUNK, TILE, dtype=F32),
            vmem(TILE, TILE),
            vmem(NZ, NX, TILE, D),
            vmem(NZ, NX, TILE, D),
            vmem(NZ, NX, TILE, D),
            vmem(NX - 1, NZ, ROWS_X, D),
            vmem(NZ, ROWS_X, D),
            vmem(NZ - 1, ROWS_X, D),
            vmem(NZ - 1, NX, ROWS_Z, D),
            vmem(NX, ROWS_Z, D),
            vmem(NX - 1, ROWS_Z, D),
            vmem(TILE, D),
            vmem(NY - 1, CHUNK, D),
            vmem(CHUNK, D, dtype=F32),
            vmem(CHUNK, D, dtype=F32),
        ]
        + [pltpu.SemaphoreType.DMA((6,))]
        + sems(192),
        compiler_params=remote(0),
    )(
        *(
            pltpu.with_memory_space_constraint(array, pltpu.HBM)
            for array in (item_features, weights, cotangent, tiles, tile_order, tile_counts)
        )
    )
    hidden, item_grad, weight_grad = pl.pallas_call(
        finish_kernel,
        out_shape=(shape(SHARE, H), shape(TILE, D, dtype=F32), shape(LEVELS * D, H, dtype=F32)),
        in_specs=[VM] * 3,
        out_specs=(VM,) * 3,
        compiler_params=pltpu.CompilerParams(vmem_limit_bytes=LIMIT),
    )(hidden, item_sum, weight_sum.reshape(NZ, LEVELS * D, TILE))
    return (hidden, item_grad, weight_grad.reshape(LEVELS, D, H))


def solution(mesh):
    in_specs = (
        P("item", None),
        P(),
        P("user", "item", None, None, None),
        P("user", None),
        P("user", None),
        P(("user", "item"), None),
    )
    out_specs = (P(("user", "item"), None), P("item", None), P())
    return jax.shard_map(
        per_device, mesh=mesh, in_specs=in_specs, out_specs=out_specs, check_vma=False
    )
```
